32 devices in a mesh: dp: 4 (over y, x), atom: 8 (over z, core).
Axes of the slice: x: 2, y: 2, z: 4, core: 2. Of those that a mesh axis runs over, the one named last changes fastest.
Arguments:
- patch_slots: bfloat16 [4, 768, 1024], P('dp', 'atom'), may hold values from -6 to 6
- slot_counts: int32 [4, 8], P('dp'), may hold values from 1 to 96, 256 in all within a row
- dictionary: bfloat16 [1024, 8192], P(None, 'atom')
Outputs:
- sparse_codes: float32 [4, 256, 8192], P('dp', None, 'atom')
- new_dictionary: float32 [1024, 8192], P('dp', 'atom')
The draws below stay inside these ranges and needn't reach their ends.
Inputs may be any that keep to these rules, and one draw needn't show every extreme that they name: `slot_counts`: each row sums to 256 and its largest entry is exactly 96; slots at or beyond a device's count are ignored.
All inputs are finite; a program needn't handle non-finite values.
Results may differ from the reference program's by a relative error of at most 0.0009.
The reference program's roundings to bfloat16 on the way (of `patches`, `code_half` and `residual`) count: a program that leaves them out, or rounds other values in their place, can miss the bound.
Values may be sent and summed in bfloat16 or wider, within the bound.
A program may use at most 64 MiB of HBM per device.

```python
import math
import jax
import jax.numpy as jnp
import numpy as np
from jax import lax

P_SIZE = 1024
B = 256
ITERS = 3
ATOMS = 8192
CAP = 96
N_DP = 4
N_ATOM = 8


def draw_dictionary(key, part):
    first, second = jax.random.split(jax.random.fold_in(key, 11))
    position = jnp.arange(ATOMS, dtype=jnp.float32) / ATOMS
    base = jax.random.normal(first, (P_SIZE, ATOMS), jnp.float32)
    spread = jax.random.uniform(second, (ATOMS,), jnp.float32, math.log(0.8), math.log(1.25))
    column_scale = jnp.exp(position * math.log(3.0) + spread)
    return (base * column_scale[None, :] / math.sqrt(P_SIZE)).astype(jnp.bfloat16)


def shard_levels(rng, dims, cuts, smallest, largest):
    def one(dim, blocks):
        heights = jax.random.uniform(jax.random.fold_in(jax.random.fold_in(rng, 6), dim), (blocks,), jnp.float32, smallest / len(cuts), largest / len(cuts))
        return jnp.repeat(jnp.exp(heights), dims[dim] // blocks).reshape((-1,) + (1,) * (len(dims) - dim - 1))

    gain = one(*cuts[0])
    for cut in cuts[1:]:
        gain = gain * one(*cut)
    return gain


def split_up(number_of, total, most, slope):
    portions = [(1 << 20) // math.isqrt(standing ** slope) + 1 for standing in range(2, number_of + 1)]
    rest, holding = total - most - (number_of - 1), [1] * (number_of - 1)
    while rest > 0:
        movable = [i for i in range(number_of - 1) if holding[i] < most]
        pool, remaining = sum([portions[i] for i in movable]), rest
        for i in movable:
            more = min(most - holding[i], max(1, remaining * portions[i] // pool), rest)
            holding[i] = holding[i] + more
            rest = rest - more
    return np.array([most] + holding)


def uneven(own_key, number_of, total, bound, skew):
    if number_of == 2:
        one = jax.random.randint(own_key, (), max(1, total - bound), min(bound, total - 1) + 1)
        return jnp.stack([one, total - one])
    tallies = jnp.asarray(split_up(number_of, total, bound, skew), jnp.int32)
    couples = (number_of - 1) // 2
    donor, receiver = tallies[1:1 + 2 * couples:2], tallies[2:2 + 2 * couples:2]
    room = jnp.minimum(donor - 1, bound - receiver)
    passed = jax.random.randint(jax.random.fold_in(own_key, 1), (couples,), 0, 1 << 20) % (room + 1)
    tallies = tallies.at[1:1 + 2 * couples:2].set(donor - passed).at[2:2 + 2 * couples:2].set(receiver + passed)
    return tallies[jax.random.permutation(jax.random.fold_in(own_key, 2), number_of)]


def centred(key, shape, scale, reach, pieces=(), kind=jnp.bfloat16):
    level = shard_levels(key, shape, pieces, -0.22, 0.18) if pieces else 1.0
    values = jax.random.normal(key, shape, jnp.float32) * scale * level
    return jnp.minimum(jnp.maximum(values, -reach), reach).astype(kind)


def setup_inputs(seed: int = 0) -> dict:
    splits = jax.random.split(jax.random.key(seed), 4)
    return {
        "patch_slots": centred(splits[0], (N_DP, N_ATOM * CAP, P_SIZE), 1.0, 6.0, ((0, 4), (1, 8))),
        "slot_counts": jax.vmap(lambda own: uneven(own, N_ATOM, B, CAP, 2))(jax.random.split(splits[1], N_DP)).reshape((N_DP, N_ATOM)).astype(jnp.int32),
        "dictionary": draw_dictionary(jax.random.fold_in(splits[3], 71), 0),
    }


def shrink(values):
    return values - jnp.clip(values, -1.0, 1.0)

def compact(slot_rows, counts):
    slot_ends = jnp.cumsum(counts).astype(jnp.int32)
    slot_starts = slot_ends - counts
    position = jnp.arange(B, dtype=jnp.int32)
    owner_index = lax.optimization_barrier(jnp.sum((slot_ends[None, :] <= position[:, None]).astype(jnp.int32), axis=1))
    start_of = slot_starts[owner_index]
    source = (owner_index * CAP + position - start_of).astype(jnp.int32)
    return slot_rows[source]

def reference(patch_slots, slot_counts, dictionary):
    lipschitz = 4.0 * (1.0 + math.sqrt(ATOMS / P_SIZE)) ** 2

    def residual_of(patches, sparse):
        code_half = sparse.astype(jnp.bfloat16)
        recon = jnp.dot(code_half, dictionary.T, preferred_element_type=jnp.float32)
        residual = (recon / lipschitz - patches.astype(jnp.float32)).astype(jnp.bfloat16)
        return (code_half, residual)

    def one_group(gradient, group):
        slot_rows, counts = group
        patches = compact(slot_rows, counts)
        sparse = shrink(jnp.dot(patches, dictionary, preferred_element_type=jnp.float32))
        for step in range(ITERS - 1):
            code_half, residual = residual_of(patches, sparse)
            sparse = shrink(sparse - jnp.dot(residual, dictionary, preferred_element_type=jnp.float32))
        code_half, residual = residual_of(patches, sparse)
        gradient = gradient + jnp.dot(residual.T, code_half, preferred_element_type=jnp.float32)
        return (gradient, sparse)
    start_grad = jnp.zeros((P_SIZE, ATOMS), jnp.float32)
    gradient, sparse_codes = lax.scan(one_group, start_grad, (patch_slots, slot_counts))
    grad_total = jnp.sum(gradient * gradient)
    step_scale = 0.5 * math.sqrt(ATOMS) / jnp.sqrt(grad_total)
    stepped = dictionary.astype(jnp.float32) - step_scale * gradient
    column_sq = lax.optimization_barrier(jnp.sum(stepped * stepped, axis=0))
    new_dictionary = stepped / jnp.sqrt(column_sq + 1e-06)[None, :]
    return (sparse_codes, new_dictionary)
```

```python
import functools
import math

import jax
import jax.numpy as jnp
from jax import lax
from jax.experimental import pallas as pl
from jax.experimental.pallas import tpu as pltpu
from jax.sharding import PartitionSpec as P

B = 256
ITERS = 3
CORES = 2
PARTS = 2
LINK = jnp.bfloat16
MESH = pl.DeviceIdType.MESH


def shrink(values):
    return values - jnp.clip(values, -1.0, 1.0)


def kernel(
    groups, chips, counts_ref, slots_ref, dict_hbm, codes_hbm, newd_ref, dict_ref, codes_ref,
    slots_all, gathered, res, half, sib_send, sib_recv, own_part, z_send, z_recv, sent_sum, recv_sum,
    patch, half_recv, rows_res, grad, tot_send, tot_line, tot_dp, col_send, col_recv,
    send_sem, recv_sem, load_sem,
):
    atoms_dev = chips * CORES
    capacity, share = slots_all.shape[1], slots_all.shape[2]
    features = atoms_dev * share
    atom_local = dict_ref.shape[3]
    atoms_total = atom_local * atoms_dev
    lipschitz = 4.0 * (1.0 + math.sqrt(atoms_total / features)) ** 2
    g = lax.axis_index("dp")
    a = lax.axis_index("atom")
    z, k = a // CORES, a % CORES
    other = 1 - k
    sib = a + 1 - 2 * k
    started = []
    span = B // PARTS

    def send(src, dst, device):
        i = len(started)
        copy = pltpu.make_async_remote_copy(
            src_ref=src, dst_ref=dst, send_sem=send_sem.at[i], recv_sem=recv_sem.at[i],
            device_id=device, device_id_type=MESH,
        )
        copy.start()
        started.append(copy)
        return copy

    load = pltpu.make_async_copy(dict_hbm, dict_ref, load_sem.at[0])
    load.start()

    def slots_of(device):
        if share % 128:
            return slots_ref.at[device]
        return slots_ref.at[:, pl.ds(pl.multiple_of(device * share, share), share)]

    keep = pltpu.make_async_copy(slots_of(a), slots_all.at[a], load_sem.at[1])
    keep.start()
    barrier = pltpu.get_barrier_semaphore()
    for r in range(1, atoms_dev):
        pl.semaphore_signal(barrier, inc=1, device_id=(g, (a + r) % atoms_dev), device_id_type=MESH)
    for q in range(1, groups):
        pl.semaphore_signal(barrier, inc=1, device_id=((g + q) % groups, a), device_id_type=MESH)
    pl.semaphore_wait(barrier, atoms_dev - 1 + groups - 1)

    moves = []
    for r in range(1, atoms_dev):
        peer = (a + r) % atoms_dev
        moves.append(send(slots_of(peer), slots_all.at[a], (g, peer)))
    row = lax.broadcasted_iota(jnp.int32, (capacity, B), 0)
    col = lax.broadcasted_iota(jnp.int32, (capacity, B), 1)
    for c in moves:
        c.wait_recv()
    keep.wait()
    acc = jnp.zeros((share, B), jnp.float32)
    start = jnp.int32(0)
    for j in range(atoms_dev):
        count = counts_ref[j]
        hit = jnp.logical_and(col - start == row, row < count)
        pick = jnp.where(hit, 1.0, 0.0).astype(jnp.bfloat16)
        acc = acc + lax.dot_general(
            slots_all[j], pick, (((0,), (0,)), ((), ())), preferred_element_type=jnp.float32
        )
        start = start + count

    tile = min(256, atom_local)
    tiles = atom_local // tile

    def along(t, h):
        return [
            send(gathered.at[t, h, a], gathered.at[t, h, a], (g, (z + r) % chips * CORES + k))
            for r in range(1, chips)
        ]

    def gather_start(t, h):
        direct = along(t, h)
        return direct, [send(gathered.at[t, h, a], gathered.at[t, h, a], (g, sib))]

    def gather_end(t, h, direct, pending):
        for r in range(1, chips):
            direct[r - 1].wait_recv()
            src = (z - r + chips) % chips * CORES + k
            pending.append(send(gathered.at[t, h, src], gathered.at[t, h, src], (g, sib)))
        for c in pending:
            c.wait_recv()

    def code(t, h):
        res[h] = gathered[t, h].reshape(features, span).T
        rows = slice(h * span, (h + 1) * span)

        def body(i, _):
            cols = pl.ds(pl.multiple_of(i * tile, tile), tile)
            d = dict_ref[:, :, :, cols].reshape(features, tile)
            prod = jnp.dot(res[h], d, preferred_element_type=jnp.float32)
            if t == 0:
                new = shrink(-prod)
            else:
                new = shrink(codes_ref[rows, cols] - prod)
            codes_ref[rows, cols] = new
            half[h, :, cols] = new.astype(jnp.bfloat16)
            return 0

        lax.fori_loop(0, tiles, body, 0)

    def partial(h, core):
        d = dict_ref[:, core].reshape(chips * share, atom_local)
        out = lax.dot_general(
            d, half[h], (((1,), (1,)), ((), ())), preferred_element_type=jnp.float32
        )
        return out.reshape(chips, share, span)

    def known(history, t, h, slot):
        if t == 1:
            return 2.0 * history[0, h, slot]
        return 2.0 * history[t - 1, h, slot] - history[t - 2, h, slot]

    order = list(range(chips - 1, -1, -1))

    def recon_start(t, h):
        sib_send[t, h] = partial(h, other)
        moves = {}
        for r in order:
            zz = (z + r) % chips
            moves[r] = send(sib_send.at[t, h, zz], sib_recv.at[t, h, zz], (g, sib))
        own_part[h] = partial(h, k)
        return moves

    def recon_mid(t, h, moves):
        arrivals = []
        mine = None
        for r in order:
            zz = (z + r) % chips
            moves[r].wait_recv()
            both = own_part[h, zz] + sib_recv[t, h, zz]
            if r == 0:
                mine = both
                continue
            dest = zz * CORES + k
            s = r - 1
            if t == 0:
                base = gathered[0, h, dest].astype(jnp.float32)
                fit = jnp.sum(both * base, axis=0, keepdims=True)
                fit = fit / (jnp.sum(base * base, axis=0, keepdims=True) + 1e-30)
                fit = fit.astype(LINK)
                z_send[t, h, s, share:] = jnp.broadcast_to(fit, (16, span))
                guess = fit.astype(jnp.float32) * base
                rows = share + 16
            else:
                guess = known(sent_sum, t, h, s)
                rows = share
            step = (both - guess).astype(LINK)
            z_send[t, h, s, :share] = step
            sent_sum[t, h, s] = guess + step.astype(jnp.float32)
            arrivals.append(
                (s, send(z_send.at[t, h, s, pl.ds(0, rows)], z_recv.at[t, h, s, pl.ds(0, rows)], (g, dest)))
            )
        return mine, arrivals

    def recon_end(t, h, mine, arrivals):
        for s, c in arrivals:
            c.wait_recv()
            if t == 0:
                guess = z_recv[t, h, s, share:share + 1].astype(jnp.float32) * (-patch[h])
            else:
                guess = known(recv_sum, t, h, s)
            value = guess + z_recv[t, h, s, :share].astype(jnp.float32)
            recv_sum[t, h, s] = value
            mine = mine + value
        gathered[t + 1, h, a] = (mine / lipschitz - patch[h]).astype(jnp.bfloat16)

    load.wait()
    gathers = []
    for h in range(PARTS):
        patch[h] = acc[:, h * span:(h + 1) * span]
        gathered[0, h, a] = (-patch[h]).astype(jnp.bfloat16)
        gathers.append(gather_start(0, h))
    half_moves = []
    square = groups == 4 and PARTS == 2
    near = [g // 2 * 2 + 1 - g % 2, (g + 2) % 4]
    sources = near + [(near[0] + 2) % 4]

    def relay(h):
        came, onward = (1, 0) if h == 0 else (0, 1)
        half_moves[2 * h + came].wait_recv()
        taken.add(2 * h + came)
        relayed.append(send(half_recv.at[came, h], half_recv.at[2, h], (near[onward], a)))

    taken, relayed, stores = set(), [], []
    for t in range(ITERS):
        last = t == ITERS - 1
        starts, mids = [], []
        for h in range(PARTS):
            gather_end(t, h, *gathers[h])
            if h > 0:
                mids.append(recon_mid(t, h - 1, starts[h - 1]))
            code(t, h)
            if last:
                rows = pl.ds(h * span, span)
                store = pltpu.make_async_copy(
                    codes_ref.at[rows], codes_hbm.at[rows], load_sem.at[2 + h]
                )
                store.start()
                stores.append(store)
            if last and square:
                for q in range(2):
                    half_moves.append(send(half.at[h], half_recv.at[q, h], (near[q], a)))
            elif last:
                for q in range(1, groups):
                    half_moves.append(
                        send(half.at[h], half_recv.at[q - 1, h], ((g + q) % groups, a))
                    )
            starts.append(recon_start(t, h))
        mids.append(recon_mid(t, PARTS - 1, starts[PARTS - 1]))
        if last and square:
            relay(0)
        gathers = []
        for h in range(PARTS):
            recon_end(t, h, *mids[h])
            gathers.append(along(t + 1, h) if last else gather_start(t + 1, h))

    if square:
        relay(1)
    over, pending = [], []
    for h in range(PARTS):
        for c in gathers[h]:
            c.wait_recv()
        for q in range(1, groups):
            d = (g + q) % groups
            over.append(send(gathered.at[ITERS, h, d * CORES + k], rows_res.at[g, h, k], (d, a)))
        rows_res[g, h, k] = gathered[ITERS, h, g * CORES + k]
        pending.append(send(rows_res.at[g, h, k], rows_res.at[g, h, k], (g, sib)))
    for h in range(PARTS):
        for q in range(1, groups):
            over[h * (groups - 1) + q - 1].wait_recv()
            src = (g - q + groups) % groups
            pending.append(send(rows_res.at[src, h, k], rows_res.at[src, h, k], (g, sib)))
    rest = [c for i, c in enumerate(half_moves) if i not in taken]
    for c in pending + rest + relayed:
        c.wait_recv()
    for q in range(groups):
        if square and q:
            src = sources[q - 1]
        else:
            src = (g - q + groups) % groups
        left = jnp.concatenate(
            [rows_res[src, h].reshape(CORES * share, span) for h in range(PARTS)], axis=1
        )
        for i in range(tiles):
            cols = slice(i * tile, (i + 1) * tile)
            right = half[:, :, cols] if q == 0 else half_recv[q - 1, :, :, cols]
            prod = jnp.dot(left, right.reshape(B, tile), preferred_element_type=jnp.float32)
            if q == 0:
                grad[:, cols] = prod
            else:
                grad[:, cols] = grad[:, cols] + prod

    value = grad[...]
    total = jnp.sum(jnp.sum(value * value, axis=0, keepdims=True), axis=1, keepdims=True)
    tot_send[0] = jnp.broadcast_to(total, tot_send.shape[1:])
    moves = []
    for r in range(1, atoms_dev):
        moves.append(send(tot_send.at[0], tot_line.at[r - 1], (g, (a + r) % atoms_dev)))
    line = tot_send[0]
    for r in range(1, atoms_dev):
        moves[r - 1].wait_recv()
        line = line + tot_line[r - 1]
    tot_send[1] = line
    moves = []
    for q in range(1, groups):
        moves.append(send(tot_send.at[1], tot_dp.at[q - 1], ((g + q) % groups, a)))
    for q in range(1, groups):
        moves[q - 1].wait_recv()
        line = line + tot_dp[q - 1]
    scale = (0.5 * math.sqrt(atoms_total)) / jnp.sqrt(line[0:1, 0:1])
    own_rows = dict_ref[g].reshape(CORES * share, atom_local).astype(jnp.float32)
    stepped = own_rows - scale * value
    grad[...] = stepped
    column = jnp.sum(stepped * stepped, axis=0, keepdims=True)
    col_send[...] = jnp.broadcast_to(column, col_send.shape)
    moves = []
    for q in range(1, groups):
        moves.append(send(col_send, col_recv.at[q - 1], ((g + q) % groups, a)))
    for q in range(1, groups):
        moves[q - 1].wait_recv()
        column = column + col_recv[q - 1, 0:1, :]
    newd_ref[...] = grad[...] / jnp.sqrt(column + 1e-06)
    for c in stores:
        c.wait()
    for c in started:
        c.wait_send()


def finish(codes_ref, newd_ref, codes_out, newd_out, sem):
    copies = [
        pltpu.make_async_copy(codes_ref, codes_out, sem.at[0]),
        pltpu.make_async_copy(newd_ref, newd_out, sem.at[1]),
    ]
    for c in copies:
        c.start()
    for c in copies:
        c.wait()


def local(groups, chips, patch_slots, slot_counts, dictionary):
    atoms_dev = chips * CORES
    slots = patch_slots[0]
    capacity, features = slots.shape
    share = features // atoms_dev
    atom_local = dictionary.shape[1]
    if share % 128:
        slots = slots.reshape(capacity, atoms_dev, share).transpose(1, 0, 2)
    blocks = dictionary.reshape(chips, CORES, share, atom_local)
    rows = CORES * share
    copies = (
        2 * (atoms_dev - 1) + 2 * (groups - 1)
        + PARTS * (2 * ITERS * (2 * chips - 1) + (chips - 1) + (groups - 1) + (2 * groups - 1))
    )
    span = B // PARTS
    bf16, f32 = jnp.bfloat16, jnp.float32
    codes, newd = pl.pallas_call(
        functools.partial(kernel, groups, chips),
        out_shape=(
            jax.ShapeDtypeStruct((B, atom_local), f32),
            jax.ShapeDtypeStruct((rows, atom_local), f32),
        ),
        in_specs=[
            pl.BlockSpec(memory_space=pltpu.SMEM),
            pl.BlockSpec(memory_space=pltpu.HBM),
            pl.BlockSpec(memory_space=pltpu.HBM),
        ],
        out_specs=(pl.BlockSpec(memory_space=pl.ANY), pl.BlockSpec(memory_space=pltpu.VMEM)),
        scratch_shapes=[
            pltpu.VMEM((chips, CORES, share, atom_local), bf16),
            pltpu.VMEM((B, atom_local), f32),
            pltpu.VMEM((atoms_dev, capacity, share), bf16),
            pltpu.VMEM((ITERS + 1, PARTS, atoms_dev, share, span), bf16),
            pltpu.VMEM((PARTS, span, features), bf16),
            pltpu.VMEM((PARTS, span, atom_local), bf16),
            pltpu.VMEM((ITERS, PARTS, chips, share, span), f32),
            pltpu.VMEM((ITERS, PARTS, chips, share, span), f32),
            pltpu.VMEM((PARTS, chips, share, span), f32),
            pltpu.VMEM((ITERS, PARTS, chips - 1, share + 16, span), LINK),
            pltpu.VMEM((ITERS, PARTS, chips - 1, share + 16, span), LINK),
            pltpu.VMEM((ITERS, PARTS, chips - 1, share, span), f32),
            pltpu.VMEM((ITERS, PARTS, chips - 1, share, span), f32),
            pltpu.VMEM((PARTS, share, span), f32),
            pltpu.VMEM((groups - 1, PARTS, span, atom_local), bf16),
            pltpu.VMEM((groups, PARTS, CORES, share, span), bf16),
            pltpu.VMEM((rows, atom_local), f32),
            pltpu.VMEM((2, 8, 128), f32),
            pltpu.VMEM((atoms_dev - 1, 8, 128), f32),
            pltpu.VMEM((groups - 1, 8, 128), f32),
            pltpu.VMEM((8, atom_local), f32),
            pltpu.VMEM((groups - 1, 8, atom_local), f32),
            pltpu.SemaphoreType.DMA((copies,)),
            pltpu.SemaphoreType.DMA((copies,)),
            pltpu.SemaphoreType.DMA((2 + PARTS,)),
        ],
        compiler_params=pltpu.CompilerParams(
            collective_id=0, has_side_effects=True, vmem_limit_bytes=44 * 1024 * 1024
        ),
    )(slot_counts[0], slots, blocks)
    codes, newd = pl.pallas_call(
        finish,
        out_shape=(
            jax.ShapeDtypeStruct(codes.shape, f32),
            jax.ShapeDtypeStruct(newd.shape, f32),
        ),
        in_specs=[pl.BlockSpec(memory_space=pl.ANY)] * 2,
        out_specs=(pl.BlockSpec(memory_space=pl.ANY),) * 2,
        scratch_shapes=[pltpu.SemaphoreType.DMA((2,))],
        compiler_params=pltpu.CompilerParams(vmem_limit_bytes=8 * 1024 * 1024),
    )(codes, newd)
    return (codes[None], newd)


def solution(mesh):
    groups = mesh.shape["dp"]
    chips = mesh.shape["atom"] // CORES
    assert chips == groups
    placed = (P("dp", "atom", None), P("dp", None), P(None, "atom"))
    return jax.shard_map(
        functools.partial(local, groups, chips),
        mesh=mesh,
        in_specs=placed,
        out_specs=(P("dp", None, "atom"), P("dp", "atom")),
        check_vma=False,
    )
```

```python
import functools
import math

import jax
import jax.numpy as jnp
from jax import lax
from jax.experimental import pallas as pl
from jax.experimental.pallas import tpu as pltpu
from jax.sharding import PartitionSpec as P

B = 256
ITERS = 3
CORES = 2
PARTS = 2
LINK = jnp.bfloat16
MESH = pl.DeviceIdType.MESH
F32 = jnp.float32
BF16 = jnp.bfloat16


def shrink(values):
    return values - jnp.clip(values, -1.0, 1.0)


def flip(index, mask, size):
    bit = 1
    while bit < size:
        if mask & bit:
            index = index + bit * (1 - 2 * ((index // bit) % 2))
        bit *= 2
    return index


def kernel(
    groups, chips, counts_ref, slots_hbm, dict_hbm, codes_out, newd_ref,
    slots, dic, dic_t, con_send, con_recv, gath, codes, half, own_part, z_send, z_recv, sent_sum, recv_sum,
    resid, half_all, stage, res_all, grad, col_send, col_recv, tot_send, tot_recv,
    send_sem, recv_sem, over_send, over_recv, load_sem,
):
    atoms_dev = chips * CORES
    capacity, features = slots.shape[1], slots.shape[2]
    share = features // chips
    atom_local = codes.shape[2]
    atoms_total = atom_local * atoms_dev
    span = half.shape[1]
    rows_core = PARTS * span
    lipschitz = 4.0 * (1.0 + math.sqrt(atoms_total / features)) ** 2
    g = lax.axis_index("dp")
    a = lax.axis_index("atom")
    z, k = a // CORES, a % CORES
    other = 1 - k
    sib = a + 1 - 2 * k
    mine_lanes = pl.ds(pl.multiple_of(k * atom_local, atom_local), atom_local)
    other_lanes = pl.ds(pl.multiple_of(other * atom_local, atom_local), atom_local)
    home = z == g
    started = []

    def send(src, dst, device):
        i = len(started)
        copy = pltpu.make_async_remote_copy(
            src_ref=src, dst_ref=dst, send_sem=send_sem.at[i], recv_sem=recv_sem.at[i],
            device_id=device, device_id_type=MESH,
        )
        copy.start()
        started.append(copy)
        return copy

    def chip_of(mask):
        return flip(z, mask, chips)

    masks = list(range(chips - 1, 0, -1))

    load_slots = pltpu.make_async_copy(slots_hbm, slots.at[k], load_sem.at[0])
    load_slots.start()
    load_dict = pltpu.make_async_copy(dict_hbm, dic.at[k], load_sem.at[1])
    load_dict.start()

    barrier = pltpu.get_barrier_semaphore()
    for r in range(1, atoms_dev):
        pl.semaphore_signal(barrier, inc=1, device_id=(g, (a + r) % atoms_dev), device_id_type=MESH)
    for q in range(1, groups):
        pl.semaphore_signal(barrier, inc=1, device_id=((g + q) % groups, a), device_id_type=MESH)
        pl.semaphore_signal(
            barrier, inc=1, device_id=((g + q) % groups, g * CORES + k), device_id_type=MESH
        )

    @pl.when(jnp.logical_not(home))
    def _():
        pl.semaphore_signal(barrier, inc=1, device_id=(g, g * CORES + k), device_id_type=MESH)

    load_slots.wait()
    pl.semaphore_wait(barrier, atoms_dev - 1 + groups - 1 + chips - jnp.where(home, 1, 0))

    swap = send(slots.at[k], slots.at[k], (g, sib))
    picks = []
    slot = lax.broadcasted_iota(jnp.int32, (span, capacity), 1)
    row = lax.broadcasted_iota(jnp.int32, (span, capacity), 0) + k * rows_core
    for j in range(CORES):
        source = z * CORES + j
        start = jnp.int32(0)
        for i in range(atoms_dev):
            start = start + jnp.where(i < source, counts_ref[i], 0)
        count = counts_ref[source]
        for h in range(PARTS):
            hit = jnp.logical_and(row + h * span - start == slot, slot < count)
            picks.append(jnp.where(hit, -1.0, 0.0).astype(BF16))
    swap.wait_recv()
    load_dict.wait()
    share_dict = send(dic.at[k], dic.at[k], (g, sib))

    contributed = []
    for h in range(PARTS):
        part = jnp.dot(picks[h], slots[0], preferred_element_type=F32)
        part = part + jnp.dot(picks[PARTS + h], slots[1], preferred_element_type=F32)
        for c in range(chips):
            con_send[h, c] = part[:, c * share:(c + 1) * share].astype(BF16)
        contributed.append([
            send(con_send.at[h, chip_of(x)], con_recv.at[h, x - 1], (g, chip_of(x) * CORES + k))
            for x in masks
        ])

    def turn(j):
        def body(c, _):
            rows = pl.ds(pl.multiple_of(j * atom_local, atom_local), atom_local)
            dic_t[c, rows, :] = dic[j, c].T
            return 0

        lax.fori_loop(0, chips, body, 0)

    def gather(t, h):
        return [
            send(gath.at[t, h, z], gath.at[t, h, z], (g, chip_of(x) * CORES + k)) for x in masks
        ]

    turn(k)
    gathers = []
    for h in range(PARTS):
        total = con_send[h, z].astype(F32)
        for c in contributed[h]:
            c.wait_recv()
        for x in masks:
            total = total + con_recv[h, x - 1].astype(F32)
        gath[0, h, z] = total.astype(BF16)
        gathers.append(gather(0, h))
    square_d = jnp.zeros((1, atom_local), F32)
    for c in range(chips):
        block = dic[k, c].astype(F32)
        square_d = square_d + jnp.sum(block * block, axis=0, keepdims=True)
    share_dict.wait_recv()
    turn(other)

    tile = min(512, atom_local)

    def code(t, h):
        rows = slice(h * span, (h + 1) * span)
        x = jnp.concatenate([gath[t, h, c] for c in range(chips)], axis=1)
        for j in range(CORES):
            for i in range(atom_local // tile):
                cols = slice(i * tile, (i + 1) * tile)
                d = dic[j, :, :, cols].reshape(features, tile)
                prod = jnp.dot(x, d, preferred_element_type=F32)
                if t == 0:
                    new = shrink(-prod)
                else:
                    new = shrink(codes[j, rows, cols] - prod)
                codes[j, rows, cols] = new
                half[h, :, j * atom_local + i * tile:j * atom_local + (i + 1) * tile] = new.astype(BF16)

    def known(history, t, h, slot):
        if t == 1:
            return 2.0 * history[0, h, slot]
        return 2.0 * history[t - 1, h, slot] - history[t - 2, h, slot]

    def recon_start(t, h):
        arrivals = []
        for x in masks:
            zz = chip_of(x)
            s = x - 1
            both = jnp.dot(half[h], dic_t[zz], preferred_element_type=F32)
            rows = span
            if t == 0:
                base = gath[0, h, zz].astype(F32)
                fit = jnp.sum(jnp.sum(both * base, axis=0, keepdims=True), axis=1, keepdims=True)
                norm = jnp.sum(jnp.sum(base * base, axis=0, keepdims=True), axis=1, keepdims=True)
                fit = (fit / (norm + 1e-30)).astype(LINK)
                z_send[t, h, s, span:] = jnp.broadcast_to(fit, (16, share))
                guess = fit.astype(F32) * base
                rows = span + 16
            else:
                guess = known(sent_sum, t, h, s)
            step = (both - guess).astype(LINK)
            z_send[t, h, s, :span] = step
            arrivals.append(
                (s, send(z_send.at[t, h, s, pl.ds(0, rows)], z_recv.at[t, h, s, pl.ds(0, rows)], (g, zz * CORES + k)))
            )
            if t < ITERS - 1:
                sent_sum[t, h, s] = guess + step.astype(F32)
        own_part[h] = jnp.dot(half[h], dic_t[z], preferred_element_type=F32)
        return arrivals

    def recon_end(t, h, arrivals):
        mine = own_part[h]
        negative = gath[0, h, z].astype(F32)
        for s, c in reversed(arrivals):
            c.wait_recv()
            if t == 0:
                guess = z_recv[t, h, s, span:span + 1].astype(F32) * negative
            else:
                guess = known(recv_sum, t, h, s)
            value = guess + z_recv[t, h, s, :span].astype(F32)
            if t < ITERS - 1:
                recv_sum[t, h, s] = value
            mine = mine + value
        return (mine / lipschitz + negative).astype(BF16)

    square = groups == 4 and PARTS == 2
    near = [g // 2 * 2 + 1 - g % 2, (g + 2) % 4]
    half_moves, relayed, to_sib, locals_ = {}, {}, [], []

    def half_start(h):
        keep = pltpu.make_async_copy(half.at[h, :, mine_lanes], half_all.at[h, g, k], load_sem.at[2 + h])
        keep.start()
        locals_.append(keep)
        rows = pl.ds(pl.multiple_of(k * rows_core + h * span, span), span)
        keep = pltpu.make_async_copy(
            codes.at[k, pl.ds(h * span, span)], codes_out.at[rows], load_sem.at[2 + PARTS + h]
        )
        keep.start()
        locals_.append(keep)
        peers = near if square else [(g + q) % groups for q in range(1, groups)]
        for i, q in enumerate(peers):
            half_moves[h, i] = (
                send(half.at[h, :, mine_lanes], half_all.at[h, g, k], (q, a)),
                send(half.at[h, :, other_lanes], stage.at[h, g], (q, a)),
            )
        to_sib.append(send(half.at[h, :, other_lanes], half_all.at[h, g, k], (g, sib)))

    def codes_start(h):
        rows = pl.ds(pl.multiple_of(k * rows_core + h * span, span), span)
        to_sib.append(send(codes.at[other, pl.ds(h * span, span)], codes_out.at[rows], (g, sib)))

    def relay(h):
        came, onward = (1, 0) if h == 0 else (0, 1)
        for c in half_moves[h, came]:
            c.wait_recv()
        source = near[came]
        relayed[h] = (
            send(half_all.at[h, source, k], half_all.at[h, source, k], (near[onward], a)),
            send(stage.at[h, source], stage.at[h, source], (near[onward], a)),
        )
        to_sib.append(send(stage.at[h, source], half_all.at[h, source, k], (g, sib)))
        for c in half_moves[h, 1 - came]:
            c.wait_recv()
        source = near[1 - came]
        to_sib.append(send(stage.at[h, source], half_all.at[h, source, k], (g, sib)))

    def half_end(h):
        if square:
            for c in relayed[h]:
                c.wait_recv()
            source = groups - 1 - g
            to_sib.append(send(stage.at[h, source], half_all.at[h, source, k], (g, sib)))
        else:
            for q in range(1, groups):
                for c in half_moves[h, q - 1]:
                    c.wait_recv()
                source = (g - q + groups) % groups
                to_sib.append(send(stage.at[h, source], half_all.at[h, source, k], (g, sib)))

    def over(h, r):
        zz = (z + r) % chips
        return pltpu.make_async_remote_copy(
            src_ref=resid.at[h], dst_ref=res_all.at[h, g, k], send_sem=over_send.at[h, r],
            recv_sem=over_recv.at[h, g], device_id=(z, zz * CORES + k), device_id_type=MESH,
        )

    def over_arrival(h, q):
        return pltpu.make_async_remote_copy(
            src_ref=resid.at[h], dst_ref=res_all.at[h, q, k], send_sem=over_send.at[h, 0],
            recv_sem=over_recv.at[h, q], device_id=(g, sib), device_id_type=MESH,
        )

    def over_start(h, value):
        resid[h] = value
        for r in range(1, chips):
            over(h, r).start()

        @pl.when(jnp.logical_not(home))
        def _():
            over(h, 0).start()

        @pl.when(home)
        def _():
            res_all[h, g, k] = value

    def over_end(h):
        for p in range(groups):
            q = (g + p) % groups
            if p:
                over_arrival(h, q).wait_recv()
            else:
                @pl.when(jnp.logical_not(home))
                def _():
                    over_arrival(h, q).wait_recv()
            to_sib.append(send(res_all.at[h, q, k], res_all.at[h, q, k], (g, sib)))

    for t in range(ITERS):
        last = t == ITERS - 1
        arrivals = []
        for h in range(PARTS):
            for c in gathers[h]:
                c.wait_recv()
            code(t, h)
            if last:
                half_start(h)
            arrivals.append(recon_start(t, h))
        gathers = []
        for h in range(PARTS):
            value = recon_end(t, h, arrivals[h])
            if last:
                over_start(h, value)
                if square:
                    relay(h)
                codes_start(h)
            else:
                gath[t + 1, h, z] = value
                gathers.append(gather(t + 1, h))

    done = 0
    cols_tile = min(256, atom_local)
    depth = groups * CORES * span
    for h in range(PARTS):
        half_end(h)
        over_end(h)
        for c in to_sib[done:]:
            c.wait_recv()
        done = len(to_sib)
        if h == 0:
            for c in locals_:
                c.wait()
        left = res_all[h].reshape(depth, share)
        for i in range(atom_local // cols_tile):
            cols = slice(i * cols_tile, (i + 1) * cols_tile)
            right = half_all[h, :, :, :, cols].reshape(depth, cols_tile)
            prod = lax.dot_general(left, right, (((0,), (0,)), ((), ())), preferred_element_type=F32)
            if h > 0:
                prod = grad[:, cols] + prod
            grad[:, cols] = prod
            if h == PARTS - 1:
                d = dic[k, g, :, cols].astype(F32)
                col_send[0:1, cols] = jnp.sum(d * prod, axis=0, keepdims=True)
                col_send[1:2, cols] = jnp.sum(prod * prod, axis=0, keepdims=True)

    moves = [send(col_send, col_recv.at[q - 1], ((g + q) % groups, a)) for q in range(1, groups)]
    column = col_send[...]
    for q in range(1, groups):
        moves[q - 1].wait_recv()
        column = column + col_recv[q - 1]
    cross, square_g = column[0:1], column[1:2]
    total = jnp.sum(square_g, axis=1, keepdims=True)
    tot_send[...] = jnp.broadcast_to(total, tot_send.shape)
    moves = [send(tot_send, tot_recv.at[r - 1], (g, (a + r) % atoms_dev)) for r in range(1, atoms_dev)]
    line = tot_send[...]
    for r in range(1, atoms_dev):
        moves[r - 1].wait_recv()
        line = line + tot_recv[r - 1]
    scale = (0.5 * math.sqrt(atoms_total)) / jnp.sqrt(line[0:1, 0:1])
    norm = square_d + scale * (scale * square_g - 2.0 * cross)
    norm = jnp.where(scale == 0.0, square_d, jnp.maximum(norm, 0.0))
    inverse = 1.0 / jnp.sqrt(norm + 1e-06)
    own_rows = dic[k, g].astype(F32)
    newd_ref[...] = (own_rows - scale * grad[...]) * inverse
    for c in started:
        c.wait_send()
    for h in range(PARTS):
        for r in range(1, chips):
            over(h, r).wait_send()

        @pl.when(jnp.logical_not(home))
        def _():
            over(h, 0).wait_send()


def finish(codes_ref, newd_ref, codes_out, newd_out, sem):
    copies = [
        pltpu.make_async_copy(codes_ref, codes_out, sem.at[0]),
        pltpu.make_async_copy(newd_ref, newd_out, sem.at[1]),
    ]
    for c in copies:
        c.start()
    for c in copies:
        c.wait()


def local(groups, chips, patch_slots, slot_counts, dictionary):
    atoms_dev = chips * CORES
    slots = patch_slots[0]
    capacity, features = slots.shape
    share = features // chips
    atom_local = dictionary.shape[1]
    blocks = dictionary.reshape(chips, share, atom_local)
    span = B // CORES // PARTS
    copies = (
        2 + 2 * ITERS * PARTS * (chips - 1) + PARTS * (2 * (groups - 1) + 3 * groups + 4)
        + (chips - 1) * PARTS + (groups - 1) + (atoms_dev - 1)
    )
    codes, newd = pl.pallas_call(
        functools.partial(kernel, groups, chips),
        out_shape=(
            pltpu.VMEM((B, atom_local), F32),
            pltpu.VMEM((share, atom_local), F32),
        ),
        in_specs=[
            pl.BlockSpec(memory_space=pltpu.SMEM),
            pl.BlockSpec(memory_space=pl.ANY),
            pl.BlockSpec(memory_space=pl.ANY),
        ],
        out_specs=(pl.BlockSpec(memory_space=pltpu.VMEM), pl.BlockSpec(memory_space=pltpu.VMEM)),
        scratch_shapes=[
            pltpu.VMEM((CORES, capacity, features), BF16),
            pltpu.VMEM((CORES, chips, share, atom_local), BF16),
            pltpu.VMEM((chips, CORES * atom_local, share), BF16),
            pltpu.VMEM((PARTS, chips, span, share), BF16),
            pltpu.VMEM((PARTS, chips - 1, span, share), BF16),
            pltpu.VMEM((ITERS, PARTS, chips, span, share), BF16),
            pltpu.VMEM((CORES, PARTS * span, atom_local), F32),
            pltpu.VMEM((PARTS, span, CORES * atom_local), BF16),
            pltpu.VMEM((PARTS, span, share), F32),
            pltpu.VMEM((ITERS, PARTS, chips - 1, span + 16, share), LINK),
            pltpu.VMEM((ITERS, PARTS, chips - 1, span + 16, share), LINK),
            pltpu.VMEM((ITERS - 1, PARTS, chips - 1, span, share), F32),
            pltpu.VMEM((ITERS - 1, PARTS, chips - 1, span, share), F32),
            pltpu.VMEM((PARTS, span, share), BF16),
            pltpu.VMEM((PARTS, groups, CORES, span, atom_local), BF16),
            pltpu.VMEM((PARTS, groups, span, atom_local), BF16),
            pltpu.VMEM((PARTS, groups, CORES, span, share), BF16),
            pltpu.VMEM((share, atom_local), F32),
            pltpu.VMEM((2, atom_local), F32),
            pltpu.VMEM((groups - 1, 2, atom_local), F32),
            pltpu.VMEM((8, 128), F32),
            pltpu.VMEM((atoms_dev - 1, 8, 128), F32),
            pltpu.SemaphoreType.DMA((copies,)),
            pltpu.SemaphoreType.DMA((copies,)),
            pltpu.SemaphoreType.DMA((PARTS, chips)),
            pltpu.SemaphoreType.DMA((PARTS, groups)),
            pltpu.SemaphoreType.DMA((2 + 2 * PARTS,)),
        ],
        compiler_params=pltpu.CompilerParams(
            collective_id=0, has_side_effects=True, vmem_limit_bytes=61 * 1024 * 1024 + 786432
        ),
    )(slot_counts[0], slots, blocks)
    codes, newd = pl.pallas_call(
        finish,
        out_shape=(
            jax.ShapeDtypeStruct((B, atom_local), F32),
            jax.ShapeDtypeStruct((share, atom_local), F32),
        ),
        in_specs=[pl.BlockSpec(memory_space=pl.ANY)] * 2,
        out_specs=(pl.BlockSpec(memory_space=pl.ANY),) * 2,
        scratch_shapes=[pltpu.SemaphoreType.DMA((2,))],
        compiler_params=pltpu.CompilerParams(vmem_limit_bytes=8 * 1024 * 1024),
    )(codes, newd)
    return (codes[None], newd)


def solution(mesh):
    groups = mesh.shape["dp"]
    chips = mesh.shape["atom"] // CORES
    assert chips == groups and chips & (chips - 1) == 0
    placed = (P("dp", "atom", None), P("dp", None), P(None, "atom"))
    return jax.shard_map(
        functools.partial(local, groups, chips),
        mesh=mesh,
        in_specs=placed,
        out_specs=(P("dp", None, "atom"), P("dp", "atom")),
        check_vma=False,
    )
```

```python
import functools
import math

import jax
import jax.numpy as jnp
from jax import lax
from jax.experimental import pallas as pl
from jax.experimental.pallas import tpu as pltpu
from jax.sharding import PartitionSpec as P

B = 256
ITERS = 3
CORES = 2
PARTS = 2
LINK = jnp.bfloat16
MESH = pl.DeviceIdType.MESH
F32 = jnp.float32
BF16 = jnp.bfloat16


def shrink(values):
    return values - jnp.clip(values, -1.0, 1.0)


def flip(index, mask, size):
    bit = 1
    while bit < size:
        if mask & bit:
            index = index + bit * (1 - 2 * ((index // bit) % 2))
        bit *= 2
    return index


def kernel(
    groups, chips, counts_ref, slots_hbm, dict_hbm, codes_out, newd_ref,
    slots, dic, dic_t, con_send, con_recv, gath, codes, half, own_part, z_send, z_recv, sent_sum, recv_sum,
    resid, half_all, stage, res_all, grad, col_send, col_recv, tot_send, tot_recv,
    send_sem, recv_sem, over_send, over_recv, load_sem,
):
    atoms_dev = chips * CORES
    capacity, features = slots.shape[1], slots.shape[2]
    share = features // chips
    atom_local = codes.shape[2]
    atoms_total = atom_local * atoms_dev
    span = half.shape[1]
    rows_core = PARTS * span
    lipschitz = 4.0 * (1.0 + math.sqrt(atoms_total / features)) ** 2
    g = lax.axis_index("dp")
    a = lax.axis_index("atom")
    z, k = a // CORES, a % CORES
    other = 1 - k
    sib = a + 1 - 2 * k
    mine_lanes = pl.ds(pl.multiple_of(k * atom_local, atom_local), atom_local)
    other_lanes = pl.ds(pl.multiple_of(other * atom_local, atom_local), atom_local)
    home = z == g
    started = []

    def send(src, dst, device):
        i = len(started)
        copy = pltpu.make_async_remote_copy(
            src_ref=src, dst_ref=dst, send_sem=send_sem.at[i], recv_sem=recv_sem.at[i],
            device_id=device, device_id_type=MESH,
        )
        copy.start()
        started.append(copy)
        return copy

    def chip_of(mask):
        return flip(z, mask, chips)

    masks = list(range(chips - 1, 0, -1))

    load_slots = pltpu.make_async_copy(slots_hbm, slots.at[k], load_sem.at[0])
    load_slots.start()
    load_dict = pltpu.make_async_copy(dict_hbm, dic.at[k], load_sem.at[1])
    load_dict.start()

    barrier = pltpu.get_barrier_semaphore()
    for r in range(1, atoms_dev):
        pl.semaphore_signal(barrier, inc=1, device_id=(g, (a + r) % atoms_dev), device_id_type=MESH)
    for q in range(1, groups):
        pl.semaphore_signal(barrier, inc=1, device_id=((g + q) % groups, a), device_id_type=MESH)
        pl.semaphore_signal(
            barrier, inc=1, device_id=((g + q) % groups, g * CORES + k), device_id_type=MESH
        )

    @pl.when(jnp.logical_not(home))
    def _():
        pl.semaphore_signal(barrier, inc=1, device_id=(g, g * CORES + k), device_id_type=MESH)

    load_slots.wait()
    pl.semaphore_wait(barrier, atoms_dev - 1 + groups - 1 + chips - jnp.where(home, 1, 0))

    swap = send(slots.at[k], slots.at[k], (g, sib))
    picks = []
    slot = lax.broadcasted_iota(jnp.int32, (span, capacity), 1)
    row = lax.broadcasted_iota(jnp.int32, (span, capacity), 0) + k * rows_core
    for j in range(CORES):
        source = z * CORES + j
        start = jnp.int32(0)
        for i in range(atoms_dev):
            start = start + jnp.where(i < source, counts_ref[i], 0)
        count = counts_ref[source]
        for h in range(PARTS):
            hit = jnp.logical_and(row + h * span - start == slot, slot < count)
            picks.append(jnp.where(hit, -1.0, 0.0).astype(BF16))
    swap.wait_recv()
    load_dict.wait()
    share_dict = send(dic.at[k], dic.at[k], (g, sib))

    contributed = []
    for h in range(PARTS):
        part = jnp.dot(picks[h], slots[0], preferred_element_type=F32)
        part = part + jnp.dot(picks[PARTS + h], slots[1], preferred_element_type=F32)
        for c in range(chips):
            con_send[h, c] = part[:, c * share:(c + 1) * share].astype(BF16)
        contributed.append([
            send(con_send.at[h, chip_of(x)], con_recv.at[h, x - 1], (g, chip_of(x) * CORES + k))
            for x in masks
        ])

    block = min(256, atom_local)
    unit = jnp.where(
        lax.broadcasted_iota(jnp.int32, (block, block), 0) == lax.broadcasted_iota(jnp.int32, (block, block), 1),
        1.0, 0.0,
    ).astype(BF16)

    def turn(j):
        for c in range(chips):
            for i in range(atom_local // block):
                rows = pl.ds(pl.multiple_of(j * atom_local + i * block, block), block)
                part = lax.dot_general(
                    unit, dic[j, c, :, i * block:(i + 1) * block], (((1,), (1,)), ((), ())),
                    preferred_element_type=F32,
                )
                dic_t[c, rows, :] = part.astype(BF16)

    def gather(t, h):
        return [
            send(gath.at[t, h, z], gath.at[t, h, z], (g, chip_of(x) * CORES + k)) for x in masks
        ]

    turn(k)
    gathers = []
    for h in range(PARTS):
        total = con_send[h, z].astype(F32)
        for c in contributed[h]:
            c.wait_recv()
        for x in masks:
            total = total + con_recv[h, x - 1].astype(F32)
        gath[0, h, z] = total.astype(BF16)
        gathers.append(gather(0, h))
    square_d = jnp.zeros((1, atom_local), F32)
    for c in range(chips):
        wide = dic[k, c].astype(F32)
        square_d = square_d + jnp.sum(wide * wide, axis=0, keepdims=True)
    share_dict.wait_recv()
    turn(other)

    tile = min(512, atom_local)

    def code(t, h):
        rows = slice(h * span, (h + 1) * span)
        x = jnp.concatenate([gath[t, h, c] for c in range(chips)], axis=1)
        for j in range(CORES):
            for i in range(atom_local // tile):
                cols = slice(i * tile, (i + 1) * tile)
                d = dic[j, :, :, cols].reshape(features, tile)
                prod = jnp.dot(x, d, preferred_element_type=F32)
                if t == 0:
                    new = shrink(-prod)
                else:
                    new = shrink(codes[j, rows, cols] - prod)
                codes[j, rows, cols] = new
                half[h, :, j * atom_local + i * tile:j * atom_local + (i + 1) * tile] = new.astype(BF16)

    def known(history, t, h, slot):
        if t == 1:
            return 2.0 * history[0, h, slot]
        return 2.0 * history[t - 1, h, slot] - history[t - 2, h, slot]

    def recon_start(t, h):
        arrivals = []
        for x in masks:
            zz = chip_of(x)
            s = x - 1
            both = jnp.dot(half[h], dic_t[zz], preferred_element_type=F32)
            rows = span
            if t == 0:
                base = gath[0, h, zz].astype(F32)
                fit = jnp.sum(jnp.sum(both * base, axis=0, keepdims=True), axis=1, keepdims=True)
                norm = jnp.sum(jnp.sum(base * base, axis=0, keepdims=True), axis=1, keepdims=True)
                fit = (fit / (norm + 1e-30)).astype(LINK)
                z_send[t, h, s, span:] = jnp.broadcast_to(fit, (16, share))
                guess = fit.astype(F32) * base
                rows = span + 16
            else:
                guess = known(sent_sum, t, h, s)
            step = (both - guess).astype(LINK)
            z_send[t, h, s, :span] = step
            arrivals.append(
                (s, send(z_send.at[t, h, s, pl.ds(0, rows)], z_recv.at[t, h, s, pl.ds(0, rows)], (g, zz * CORES + k)))
            )
            if t < ITERS - 1:
                sent_sum[t, h, s] = guess + step.astype(F32)
        own_part[h] = jnp.dot(half[h], dic_t[z], preferred_element_type=F32)
        return arrivals

    def recon_end(t, h, arrivals):
        mine = own_part[h]
        negative = gath[0, h, z].astype(F32)
        for s, c in reversed(arrivals):
            c.wait_recv()
            if t == 0:
                guess = z_recv[t, h, s, span:span + 1].astype(F32) * negative
            else:
                guess = known(recv_sum, t, h, s)
            value = guess + z_recv[t, h, s, :span].astype(F32)
            if t < ITERS - 1:
                recv_sum[t, h, s] = value
            mine = mine + value
        return (mine / lipschitz + negative).astype(BF16)

    square = groups == 4
    near = [g // 2 * 2 + 1 - g % 2, (g + 2) % 4]
    half_moves, relayed, to_sib, locals_ = {}, {}, [], []

    def half_start(h):
        keep = pltpu.make_async_copy(half.at[h, :, mine_lanes], half_all.at[h, g, k], load_sem.at[2 + h])
        keep.start()
        locals_.append(keep)
        rows = pl.ds(pl.multiple_of(k * rows_core + h * span, span), span)
        keep = pltpu.make_async_copy(
            codes.at[k, pl.ds(h * span, span)], codes_out.at[rows], load_sem.at[2 + PARTS + h]
        )
        keep.start()
        locals_.append(keep)
        peers = near if square else [(g + q) % groups for q in range(1, groups)]
        for i, q in enumerate(peers):
            half_moves[h, i] = (
                send(half.at[h, :, mine_lanes], half_all.at[h, g, k], (q, a)),
                send(half.at[h, :, other_lanes], stage.at[h, g], (q, a)),
            )
        to_sib.append(send(half.at[h, :, other_lanes], half_all.at[h, g, k], (g, sib)))

    def codes_start(h):
        rows = pl.ds(pl.multiple_of(k * rows_core + h * span, span), span)
        to_sib.append(send(codes.at[other, pl.ds(h * span, span)], codes_out.at[rows], (g, sib)))

    def relay(h):
        pieces = (half_all.at[h, near[1], k], stage.at[h, near[0]])
        relayed[h] = []
        for p in range(2):
            half_moves[h, 1 - p][p].wait_recv()
            relayed[h].append(send(pieces[p], pieces[p], (near[p], a)))
        to_sib.append(send(stage.at[h, near[0]], half_all.at[h, near[0], k], (g, sib)))
        for p in range(2):
            half_moves[h, p][p].wait_recv()
        to_sib.append(send(stage.at[h, near[1]], half_all.at[h, near[1], k], (g, sib)))

    def half_end(h):
        if square:
            for c in relayed[h]:
                c.wait_recv()
            source = groups - 1 - g
            to_sib.append(send(stage.at[h, source], half_all.at[h, source, k], (g, sib)))
        else:
            for q in range(1, groups):
                for c in half_moves[h, q - 1]:
                    c.wait_recv()
                source = (g - q + groups) % groups
                to_sib.append(send(stage.at[h, source], half_all.at[h, source, k], (g, sib)))

    def over(h, r):
        zz = (z + r) % chips
        return pltpu.make_async_remote_copy(
            src_ref=resid.at[h], dst_ref=res_all.at[h, g, k], send_sem=over_send.at[h, r],
            recv_sem=over_recv.at[h, g], device_id=(z, zz * CORES + k), device_id_type=MESH,
        )

    def over_arrival(h, q):
        return pltpu.make_async_remote_copy(
            src_ref=resid.at[h], dst_ref=res_all.at[h, q, k], send_sem=over_send.at[h, 0],
            recv_sem=over_recv.at[h, q], device_id=(g, sib), device_id_type=MESH,
        )

    def over_start(h, value):
        resid[h] = value
        for r in range(1, chips):
            over(h, r).start()

        @pl.when(jnp.logical_not(home))
        def _():
            over(h, 0).start()

        @pl.when(home)
        def _():
            res_all[h, g, k] = value

    def over_end(h):
        for p in range(groups):
            q = (g + p) % groups
            if p:
                over_arrival(h, q).wait_recv()
            else:
                @pl.when(jnp.logical_not(home))
                def _():
                    over_arrival(h, q).wait_recv()
            to_sib.append(send(res_all.at[h, q, k], res_all.at[h, q, k], (g, sib)))

    for t in range(ITERS):
        last = t == ITERS - 1
        arrivals = []
        for h in range(PARTS):
            for c in gathers[h]:
                c.wait_recv()
            code(t, h)
            if last:
                half_start(h)
            arrivals.append(recon_start(t, h))
        gathers = []
        for h in range(PARTS):
            value = recon_end(t, h, arrivals[h])
            if last:
                over_start(h, value)
                if square:
                    relay(h)
                codes_start(h)
            else:
                gath[t + 1, h, z] = value
                gathers.append(gather(t + 1, h))

    done = 0
    cols_tile = min(256, atom_local)
    depth = groups * CORES * span
    for h in range(PARTS):
        half_end(h)
        over_end(h)
        for c in to_sib[done:]:
            c.wait_recv()
        done = len(to_sib)
        if h == 0:
            for c in locals_:
                c.wait()
        left = res_all[h].reshape(depth, share)
        for i in range(atom_local // cols_tile):
            cols = slice(i * cols_tile, (i + 1) * cols_tile)
            right = half_all[h, :, :, :, cols].reshape(depth, cols_tile)
            prod = lax.dot_general(left, right, (((0,), (0,)), ((), ())), preferred_element_type=F32)
            if h > 0:
                prod = grad[:, cols] + prod
            grad[:, cols] = prod
            if h == PARTS - 1:
                d = dic[k, g, :, cols].astype(F32)
                col_send[0:1, cols] = jnp.sum(d * prod, axis=0, keepdims=True)
                col_send[1:2, cols] = jnp.sum(prod * prod, axis=0, keepdims=True)

    total = jnp.sum(col_send[1:2], axis=1, keepdims=True)
    tot_send[...] = jnp.broadcast_to(total, tot_send.shape)
    moves = [send(col_send, col_recv.at[q - 1], ((g + q) % groups, a)) for q in range(1, groups)]
    everyone = [(q, r) for q in range(groups) for r in range(atoms_dev) if q or r]
    everyone.sort(key=lambda p: abs(p[1] - atoms_dev // 2))
    totals = [
        send(tot_send, tot_recv.at[i], ((g + q) % groups, (a + r) % atoms_dev))
        for i, (q, r) in enumerate(everyone)
    ]
    column = col_send[...]
    for q in range(1, groups):
        moves[q - 1].wait_recv()
        column = column + col_recv[q - 1]
    cross, square_g = column[0:1], column[1:2]
    for c in totals:
        c.wait_recv()
    line = tot_send[...] + jnp.sum(tot_recv[...], axis=0)
    scale = (0.5 * math.sqrt(atoms_total)) / jnp.sqrt(line[0:1, 0:1])
    norm = square_d + scale * (scale * square_g - 2.0 * cross)
    norm = jnp.where(scale == 0.0, square_d, jnp.maximum(norm, 0.0))
    inverse = 1.0 / jnp.sqrt(norm + 1e-06)
    own_rows = dic[k, g].astype(F32)
    newd_ref[...] = (own_rows - scale * grad[...]) * inverse
    for c in started:
        c.wait_send()
    for h in range(PARTS):
        for r in range(1, chips):
            over(h, r).wait_send()

        @pl.when(jnp.logical_not(home))
        def _():
            over(h, 0).wait_send()


def finish(codes_ref, newd_ref, codes_out, newd_out, sem):
    copies = [
        pltpu.make_async_copy(codes_ref, codes_out, sem.at[0]),
        pltpu.make_async_copy(newd_ref, newd_out, sem.at[1]),
    ]
    for c in copies:
        c.start()
    for c in copies:
        c.wait()


def local(groups, chips, patch_slots, slot_counts, dictionary):
    atoms_dev = chips * CORES
    slots = patch_slots[0]
    capacity, features = slots.shape
    share = features // chips
    atom_local = dictionary.shape[1]
    blocks = dictionary.reshape(chips, share, atom_local)
    span = B // CORES // PARTS
    copies = (
        2 + 2 * ITERS * PARTS * (chips - 1) + PARTS * (2 * (groups - 1) + 3 * groups + 4)
        + (chips - 1) * PARTS + (groups - 1) + (groups * atoms_dev - 1)
    )
    codes, newd = pl.pallas_call(
        functools.partial(kernel, groups, chips),
        out_shape=(
            pltpu.VMEM((B, atom_local), F32),
            pltpu.VMEM((share, atom_local), F32),
        ),
        in_specs=[
            pl.BlockSpec(memory_space=pltpu.SMEM),
            pl.BlockSpec(memory_space=pl.ANY),
            pl.BlockSpec(memory_space=pl.ANY),
        ],
        out_specs=(pl.BlockSpec(memory_space=pltpu.VMEM), pl.BlockSpec(memory_space=pltpu.VMEM)),
        scratch_shapes=[
            pltpu.VMEM((CORES, capacity, features), BF16),
            pltpu.VMEM((CORES, chips, share, atom_local), BF16),
            pltpu.VMEM((chips, CORES * atom_local, share), BF16),
            pltpu.VMEM((PARTS, chips, span, share), BF16),
            pltpu.VMEM((PARTS, chips - 1, span, share), BF16),
            pltpu.VMEM((ITERS, PARTS, chips, span, share), BF16),
            pltpu.VMEM((CORES, PARTS * span, atom_local), F32),
            pltpu.VMEM((PARTS, span, CORES * atom_local), BF16),
            pltpu.VMEM((PARTS, span, share), F32),
            pltpu.VMEM((ITERS, PARTS, chips - 1, span + 16, share), LINK),
            pltpu.VMEM((ITERS, PARTS, chips - 1, span + 16, share), LINK),
            pltpu.VMEM((ITERS - 1, PARTS, chips - 1, span, share), F32),
            pltpu.VMEM((ITERS - 1, PARTS, chips - 1, span, share), F32),
            pltpu.VMEM((PARTS, span, share), BF16),
            pltpu.VMEM((PARTS, groups, CORES, span, atom_local), BF16),
            pltpu.VMEM((PARTS, groups, span, atom_local), BF16),
            pltpu.VMEM((PARTS, groups, CORES, span, share), BF16),
            pltpu.VMEM((share, atom_local), F32),
            pltpu.VMEM((2, atom_local), F32),
            pltpu.VMEM((groups - 1, 2, atom_local), F32),
            pltpu.VMEM((1, 128), F32),
            pltpu.VMEM((groups * atoms_dev - 1, 1, 128), F32),
            pltpu.SemaphoreType.DMA((copies,)),
            pltpu.SemaphoreType.DMA((copies,)),
            pltpu.SemaphoreType.DMA((PARTS, chips)),
            pltpu.SemaphoreType.DMA((PARTS, groups)),
            pltpu.SemaphoreType.DMA((2 + 2 * PARTS,)),
        ],
        compiler_params=pltpu.CompilerParams(
            collective_id=0, has_side_effects=True, vmem_limit_bytes=61 * 1024 * 1024 + 786432
        ),
    )(slot_counts[0], slots, blocks)
    codes, newd = pl.pallas_call(
        finish,
        out_shape=(
            jax.ShapeDtypeStruct((B, atom_local), F32),
            jax.ShapeDtypeStruct((share, atom_local), F32),
        ),
        in_specs=[pl.BlockSpec(memory_space=pl.ANY)] * 2,
        out_specs=(pl.BlockSpec(memory_space=pl.ANY),) * 2,
        scratch_shapes=[pltpu.SemaphoreType.DMA((2,))],
        compiler_params=pltpu.CompilerParams(vmem_limit_bytes=8 * 1024 * 1024),
    )(codes, newd)
    return (codes[None], newd)


def solution(mesh):
    groups = mesh.shape["dp"]
    chips = mesh.shape["atom"] // CORES
    assert chips == groups and chips & (chips - 1) == 0
    placed = (P("dp", "atom", None), P("dp", None), P(None, "atom"))
    return jax.shard_map(
        functools.partial(local, groups, chips),
        mesh=mesh,
        in_specs=placed,
        out_specs=(P("dp", None, "atom"), P("dp", "atom")),
        check_vma=False,
    )
```

```python
import functools
import math

import jax
import jax.numpy as jnp
from jax import lax
from jax.experimental import pallas as pl
from jax.experimental.pallas import tpu as pltpu
from jax.sharding import PartitionSpec as P

B = 256
ITERS = 3
CORES = 2
PARTS = 2
LINK = jnp.bfloat16
MESH = pl.DeviceIdType.MESH
F32 = jnp.float32
BF16 = jnp.bfloat16


def shrink(values):
    return values - jnp.clip(values, -1.0, 1.0)


def flip(index, mask, size):
    bit = 1
    while bit < size:
        if mask & bit:
            index = index + bit * (1 - 2 * ((index // bit) % 2))
        bit *= 2
    return index


def kernel(
    groups, chips, counts_ref, slots_hbm, dict_hbm, codes_out, newd_ref,
    slots, dic, dic_t, con_send, con_recv, gath, codes, half, own_part, z_send, z_recv, sent_sum, recv_sum,
    resid, half_all, res_all, grad, col_send, col_recv, tot_send, tot_recv,
    send_sem, recv_sem, over_send, over_recv, load_sem,
):
    atoms_dev = chips * CORES
    capacity, features = slots.shape[1], slots.shape[2]
    share = features // chips
    atom_local = codes.shape[2]
    atoms_total = atom_local * atoms_dev
    span = half.shape[1]
    rows_core = PARTS * span
    lipschitz = 4.0 * (1.0 + math.sqrt(atoms_total / features)) ** 2
    g = lax.axis_index("dp")
    a = lax.axis_index("atom")
    z, k = a // CORES, a % CORES
    other = 1 - k
    sib = a + 1 - 2 * k
    mine_lanes = pl.ds(pl.multiple_of(k * atom_local, atom_local), atom_local)
    other_lanes = pl.ds(pl.multiple_of(other * atom_local, atom_local), atom_local)
    home = z == g
    started = []
    emptied = []

    def send(src, dst, device):
        i = len(started)
        copy = pltpu.make_async_remote_copy(
            src_ref=src, dst_ref=dst, send_sem=send_sem.at[i], recv_sem=recv_sem.at[i],
            device_id=device, device_id_type=MESH,
        )
        copy.start()
        started.append(copy)
        return copy

    def chip_of(mask):
        return flip(z, mask, chips)

    masks = list(range(chips - 1, 0, -1))

    load_slots = pltpu.make_async_copy(slots_hbm, slots.at[k], load_sem.at[0])
    load_slots.start()
    load_dict = pltpu.make_async_copy(dict_hbm, dic.at[k], load_sem.at[1])
    load_dict.start()

    barrier = pltpu.get_barrier_semaphore()
    for r in range(1, atoms_dev):
        pl.semaphore_signal(barrier, inc=1, device_id=(g, (a + r) % atoms_dev), device_id_type=MESH)
    for q in range(1, groups):
        pl.semaphore_signal(barrier, inc=1, device_id=((g + q) % groups, a), device_id_type=MESH)
        pl.semaphore_signal(
            barrier, inc=1, device_id=((g + q) % groups, g * CORES + k), device_id_type=MESH
        )

    @pl.when(jnp.logical_not(home))
    def _():
        pl.semaphore_signal(barrier, inc=1, device_id=(g, g * CORES + k), device_id_type=MESH)

    load_slots.wait()
    pl.semaphore_wait(barrier, atoms_dev - 1 + groups - 1 + chips - jnp.where(home, 1, 0))

    swap = send(slots.at[k], slots.at[k], (g, sib))
    picks = []
    slot = lax.broadcasted_iota(jnp.int32, (span, capacity), 1)
    row = lax.broadcasted_iota(jnp.int32, (span, capacity), 0) + k * rows_core
    for j in range(CORES):
        source = z * CORES + j
        start = jnp.int32(0)
        for i in range(atoms_dev):
            start = start + jnp.where(i < source, counts_ref[i], 0)
        count = counts_ref[source]
        for h in range(PARTS):
            hit = jnp.logical_and(row + h * span - start == slot, slot < count)
            picks.append(jnp.where(hit, -1.0, 0.0).astype(BF16))
    swap.wait_recv()
    load_dict.wait()
    share_dict = send(dic.at[k], dic.at[k], (g, sib))

    contributed = []
    for h in range(PARTS):
        part = jnp.dot(picks[h], slots[0], preferred_element_type=F32)
        part = part + jnp.dot(picks[PARTS + h], slots[1], preferred_element_type=F32)
        for c in range(chips):
            con_send[h, c] = part[:, c * share:(c + 1) * share].astype(BF16)
        if h:
            for c in contributed[h - 1]:
                c.wait_send()
                emptied.append(id(c))
        contributed.append([
            send(con_send.at[h, chip_of(x)], con_recv.at[h, x - 1], (g, chip_of(x) * CORES + k))
            for x in masks
        ])

    block = min(256, atom_local)
    unit = jnp.where(
        lax.broadcasted_iota(jnp.int32, (block, block), 0) == lax.broadcasted_iota(jnp.int32, (block, block), 1),
        1.0, 0.0,
    ).astype(BF16)

    def turn(j):
        for c in range(chips):
            for i in range(atom_local // block):
                rows = pl.ds(pl.multiple_of(j * atom_local + i * block, block), block)
                part = lax.dot_general(
                    unit, dic[j, c, :, i * block:(i + 1) * block], (((1,), (1,)), ((), ())),
                    preferred_element_type=F32,
                )
                dic_t[c, rows, :] = part.astype(BF16)

    def gather(t, h):
        return [
            send(gath.at[t, h, z], gath.at[t, h, z], (g, chip_of(x) * CORES + k)) for x in masks
        ]

    turn(k)
    gathers = []
    for h in range(PARTS):
        total = con_send[h, z].astype(F32)
        for c in contributed[h]:
            c.wait_recv()
        for x in masks:
            total = total + con_recv[h, x - 1].astype(F32)
        gath[0, h, z] = total.astype(BF16)
        gathers.append(gather(0, h))
    square_d = jnp.zeros((1, atom_local), F32)
    for c in range(chips):
        wide = dic[k, c].astype(F32)
        square_d = square_d + jnp.sum(wide * wide, axis=0, keepdims=True)
    share_dict.wait_recv()
    turn(other)

    tile = min(512, atom_local)

    def code(t, h):
        rows = slice(h * span, (h + 1) * span)
        x = jnp.concatenate([gath[t, h, c] for c in range(chips)], axis=1)
        for j in range(CORES):
            for i in range(atom_local // tile):
                cols = slice(i * tile, (i + 1) * tile)
                d = dic[j, :, :, cols].reshape(features, tile)
                prod = jnp.dot(x, d, preferred_element_type=F32)
                if t == 0:
                    new = shrink(-prod)
                else:
                    new = shrink(codes[j, rows, cols] - prod)
                codes[j, rows, cols] = new
                half[h, :, j * atom_local + i * tile:j * atom_local + (i + 1) * tile] = new.astype(BF16)

    def known(history, t, h, slot):
        if t == 1:
            return 2.0 * history[0, h, slot]
        return 2.0 * history[t - 1, h, slot] - history[t - 2, h, slot]

    def recon_start(t, h):
        arrivals = []
        for x in masks:
            zz = chip_of(x)
            s = x - 1
            both = jnp.dot(half[h], dic_t[zz], preferred_element_type=F32)
            rows = span
            if t == 0:
                base = gath[0, h, zz].astype(F32)
                fit = jnp.sum(jnp.sum(both * base, axis=0, keepdims=True), axis=1, keepdims=True)
                norm = jnp.sum(jnp.sum(base * base, axis=0, keepdims=True), axis=1, keepdims=True)
                fit = (fit / (norm + 1e-30)).astype(LINK)
                z_send[t, h, s, span:] = jnp.broadcast_to(fit, (16, share))
                guess = fit.astype(F32) * base
                rows = span + 16
            else:
                guess = known(sent_sum, t, h, s)
            step = (both - guess).astype(LINK)
            z_send[t, h, s, :span] = step
            arrivals.append(
                (s, send(z_send.at[t, h, s, pl.ds(0, rows)], z_recv.at[t, h, s, pl.ds(0, rows)], (g, zz * CORES + k)))
            )
            if t < ITERS - 1:
                sent_sum[t, h, s] = guess + step.astype(F32)
        own_part[h] = jnp.dot(half[h], dic_t[z], preferred_element_type=F32)
        return arrivals

    def recon_end(t, h, arrivals):
        mine = own_part[h]
        negative = gath[0, h, z].astype(F32)
        for s, c in reversed(arrivals):
            c.wait_recv()
            if t == 0:
                guess = z_recv[t, h, s, span:span + 1].astype(F32) * negative
            else:
                guess = known(recv_sum, t, h, s)
            value = guess + z_recv[t, h, s, :span].astype(F32)
            if t < ITERS - 1:
                recv_sum[t, h, s] = value
            mine = mine + value
        return (mine / lipschitz + negative).astype(BF16)

    square = groups == 4
    near = [g // 2 * 2 + 1 - g % 2, (g + 2) % 4]
    half_moves, relayed, to_sib, locals_ = {}, {}, [], []

    def half_start(h):
        keep = pltpu.make_async_copy(half.at[h, :, mine_lanes], half_all.at[h, g, k], load_sem.at[2 + h])
        keep.start()
        locals_.append(keep)
        rows = pl.ds(pl.multiple_of(k * rows_core + h * span, span), span)
        keep = pltpu.make_async_copy(
            codes.at[k, pl.ds(h * span, span)], codes_out.at[rows], load_sem.at[2 + PARTS + h]
        )
        keep.start()
        locals_.append(keep)
        peers = near if square else [(g + q) % groups for q in range(1, groups)]
        for first in (True, False):
            for i, q in enumerate(peers):
                p = 1 - i % 2 if first else i % 2
                lanes, core = ((mine_lanes, a), (other_lanes, sib))[p]
                half_moves.setdefault((h, i), {})[p] = send(
                    half.at[h, :, lanes], half_all.at[h, g, k], (q, core)
                )
        to_sib.append(send(half.at[h, :, other_lanes], half_all.at[h, g, k], (g, sib)))

    def codes_start(h):
        rows = pl.ds(pl.multiple_of(k * rows_core + h * span, span), span)
        to_sib.append(send(codes.at[other, pl.ds(h * span, span)], codes_out.at[rows], (g, sib)))

    def relay(h):
        relayed[h] = []
        for p in range(2):
            half_moves[h, 1 - p][p].wait_recv()
            piece = half_all.at[h, near[1 - p], k if p == 0 else other]
            relayed[h].append(send(piece, piece, (near[p], a)))

    def half_end(h):
        if square:
            for p in range(2):
                half_moves[h, p][p].wait_recv()
                relayed[h][p].wait_recv()
        else:
            for q in range(1, groups):
                for c in half_moves[h, q - 1].values():
                    c.wait_recv()

    def over(h, r):
        zz = (z + r) % chips
        return pltpu.make_async_remote_copy(
            src_ref=resid.at[h], dst_ref=res_all.at[h, g, k], send_sem=over_send.at[h, r],
            recv_sem=over_recv.at[h, g], device_id=(z, zz * CORES + k), device_id_type=MESH,
        )

    def over_arrival(h, q):
        return pltpu.make_async_remote_copy(
            src_ref=resid.at[h], dst_ref=res_all.at[h, q, k], send_sem=over_send.at[h, 0],
            recv_sem=over_recv.at[h, q], device_id=(g, sib), device_id_type=MESH,
        )

    def over_start(h, value):
        resid[h] = value
        for r in range(1, chips):
            over(h, r).start()

        @pl.when(jnp.logical_not(home))
        def _():
            over(h, 0).start()

        @pl.when(home)
        def _():
            res_all[h, g, k] = value

    def over_end(h):
        for p in range(groups):
            q = (g + p) % groups
            if p:
                over_arrival(h, q).wait_recv()
            else:
                @pl.when(jnp.logical_not(home))
                def _():
                    over_arrival(h, q).wait_recv()
            to_sib.append(send(res_all.at[h, q, k], res_all.at[h, q, k], (g, sib)))

    for t in range(ITERS):
        last = t == ITERS - 1
        arrivals = []
        for h in range(PARTS):
            for c in gathers[h]:
                c.wait_recv()
            code(t, h)
            if last:
                half_start(h)
            arrivals.append(recon_start(t, h))
        gathers = []
        for h in range(PARTS):
            value = recon_end(t, h, arrivals[h])
            if last:
                over_start(h, value)
                if square:
                    relay(h)
                codes_start(h)
            else:
                gath[t + 1, h, z] = value
                gathers.append(gather(t + 1, h))

    done = 0
    cols_tile = min(256, atom_local)
    depth = groups * CORES * span
    for h in range(PARTS):
        half_end(h)
        over_end(h)
        for c in to_sib[done:]:
            c.wait_recv()
        done = len(to_sib)
        if h == 0:
            for c in locals_:
                c.wait()
        left = res_all[h].reshape(depth, share)
        for i in range(atom_local // cols_tile):
            cols = slice(i * cols_tile, (i + 1) * cols_tile)
            right = half_all[h, :, :, :, cols].reshape(depth, cols_tile)
            prod = lax.dot_general(left, right, (((0,), (0,)), ((), ())), preferred_element_type=F32)
            if h > 0:
                prod = grad[:, cols] + prod
            grad[:, cols] = prod
            if h == PARTS - 1:
                d = dic[k, g, :, cols].astype(F32)
                col_send[0:1, cols] = jnp.sum(d * prod, axis=0, keepdims=True)
                col_send[1:2, cols] = jnp.sum(prod * prod, axis=0, keepdims=True)

    total = jnp.sum(col_send[1:2], axis=1, keepdims=True)
    tot_send[...] = jnp.broadcast_to(total, tot_send.shape)
    moves = [send(col_send, col_recv.at[q - 1], ((g + q) % groups, a)) for q in range(1, groups)]
    everyone = [(q, r) for q in range(groups) for r in range(atoms_dev) if q or r]
    everyone.sort(key=lambda p: abs(p[1] - atoms_dev // 2))
    totals = [
        send(tot_send, tot_recv.at[i], ((g + q) % groups, (a + r) % atoms_dev))
        for i, (q, r) in enumerate(everyone)
    ]
    column = col_send[...]
    for q in range(1, groups):
        moves[q - 1].wait_recv()
        column = column + col_recv[q - 1]
    cross, square_g = column[0:1], column[1:2]
    for c in totals:
        c.wait_recv()
    line = tot_send[...] + jnp.sum(tot_recv[...], axis=0)
    scale = (0.5 * math.sqrt(atoms_total)) / jnp.sqrt(line[0:1, 0:1])
    norm = square_d + scale * (scale * square_g - 2.0 * cross)
    norm = jnp.where(scale == 0.0, square_d, jnp.maximum(norm, 0.0))
    inverse = 1.0 / jnp.sqrt(norm + 1e-06)
    own_rows = dic[k, g].astype(F32)
    newd_ref[...] = (own_rows - scale * grad[...]) * inverse
    for c in started:
        if id(c) not in emptied:
            c.wait_send()
    for h in range(PARTS):
        for r in range(1, chips):
            over(h, r).wait_send()

        @pl.when(jnp.logical_not(home))
        def _():
            over(h, 0).wait_send()


def finish(codes_ref, newd_ref, codes_out, newd_out, sem):
    copies = [
        pltpu.make_async_copy(codes_ref, codes_out, sem.at[0]),
        pltpu.make_async_copy(newd_ref, newd_out, sem.at[1]),
    ]
    for c in copies:
        c.start()
    for c in copies:
        c.wait()


def local(groups, chips, patch_slots, slot_counts, dictionary):
    atoms_dev = chips * CORES
    slots = patch_slots[0]
    capacity, features = slots.shape
    share = features // chips
    atom_local = dictionary.shape[1]
    blocks = dictionary.reshape(chips, share, atom_local)
    span = B // CORES // PARTS
    copies = (
        2 + 2 * ITERS * PARTS * (chips - 1) + PARTS * (2 * (groups - 1) + groups + 4)
        + (chips - 1) * PARTS + (groups - 1) + (groups * atoms_dev - 1)
    )
    codes, newd = pl.pallas_call(
        functools.partial(kernel, groups, chips),
        out_shape=(
            pltpu.VMEM((B, atom_local), F32),
            pltpu.VMEM((share, atom_local), F32),
        ),
        in_specs=[
            pl.BlockSpec(memory_space=pltpu.SMEM),
            pl.BlockSpec(memory_space=pl.ANY),
            pl.BlockSpec(memory_space=pl.ANY),
        ],
        out_specs=(pl.BlockSpec(memory_space=pltpu.VMEM), pl.BlockSpec(memory_space=pltpu.VMEM)),
        scratch_shapes=[
            pltpu.VMEM((CORES, capacity, features), BF16),
            pltpu.VMEM((CORES, chips, share, atom_local), BF16),
            pltpu.VMEM((chips, CORES * atom_local, share), BF16),
            pltpu.VMEM((PARTS, chips, span, share), BF16),
            pltpu.VMEM((PARTS, chips - 1, span, share), BF16),
            pltpu.VMEM((ITERS, PARTS, chips, span, share), BF16),
            pltpu.VMEM((CORES, PARTS * span, atom_local), F32),
            pltpu.VMEM((PARTS, span, CORES * atom_local), BF16),
            pltpu.VMEM((PARTS, span, share), F32),
            pltpu.VMEM((ITERS, PARTS, chips - 1, span + 16, share), LINK),
            pltpu.VMEM((ITERS, PARTS, chips - 1, span + 16, share), LINK),
            pltpu.VMEM((ITERS - 1, PARTS, chips - 1, span, share), F32),
            pltpu.VMEM((ITERS - 1, PARTS, chips - 1, span, share), F32),
            pltpu.VMEM((PARTS, span, share), BF16),
            pltpu.VMEM((PARTS, groups, CORES, span, atom_local), BF16),
            pltpu.VMEM((PARTS, groups, CORES, span, share), BF16),
            pltpu.VMEM((share, atom_local), F32),
            pltpu.VMEM((2, atom_local), F32),
            pltpu.VMEM((groups - 1, 2, atom_local), F32),
            pltpu.VMEM((1, 128), F32),
            pltpu.VMEM((groups * atoms_dev - 1, 1, 128), F32),
            pltpu.SemaphoreType.DMA((copies,)),
            pltpu.SemaphoreType.DMA((copies,)),
            pltpu.SemaphoreType.DMA((PARTS, chips)),
            pltpu.SemaphoreType.DMA((PARTS, groups)),
            pltpu.SemaphoreType.DMA((2 + 2 * PARTS,)),
        ],
        compiler_params=pltpu.CompilerParams(
            collective_id=0, has_side_effects=True, vmem_limit_bytes=61 * 1024 * 1024 + 786432
        ),
    )(slot_counts[0], slots, blocks)
    codes, newd = pl.pallas_call(
        finish,
        out_shape=(
            jax.ShapeDtypeStruct((B, atom_local), F32),
            jax.ShapeDtypeStruct((share, atom_local), F32),
        ),
        in_specs=[pl.BlockSpec(memory_space=pl.ANY)] * 2,
        out_specs=(pl.BlockSpec(memory_space=pl.ANY),) * 2,
        scratch_shapes=[pltpu.SemaphoreType.DMA((2,))],
        compiler_params=pltpu.CompilerParams(vmem_limit_bytes=8 * 1024 * 1024),
    )(codes, newd)
    return (codes[None], newd)


def solution(mesh):
    groups = mesh.shape["dp"]
    chips = mesh.shape["atom"] // CORES
    assert chips == groups and chips & (chips - 1) == 0
    placed = (P("dp", "atom", None), P("dp", None), P(None, "atom"))
    return jax.shard_map(
        functools.partial(local, groups, chips),
        mesh=mesh,
        in_specs=placed,
        out_specs=(P("dp", None, "atom"), P("dp", "atom")),
        check_vma=False,
    )
```

```python
import functools
import math

import jax
import jax.numpy as jnp
from jax import lax
from jax.experimental import pallas as pl
from jax.experimental.pallas import tpu as pltpu
from jax.sharding import PartitionSpec as P

B = 256
ITERS = 3
CORES = 2
PARTS = 2
LINK = jnp.bfloat16
MESH = pl.DeviceIdType.MESH
F32 = jnp.float32
BF16 = jnp.bfloat16


def shrink(values):
    return values - jnp.clip(values, -1.0, 1.0)


def flip(index, mask, size):
    bit = 1
    while bit < size:
        if mask & bit:
            index = index + bit * (1 - 2 * ((index // bit) % 2))
        bit *= 2
    return index


def kernel(
    groups, chips, counts_ref, slots_hbm, dict_hbm, codes_out, newd_ref,
    slots, dic, dic_t, con_send, con_recv, gath, codes, half, own_part, z_send, z_recv, sent_sum, recv_sum,
    resid, half_all, res_all, grad, col_send, col_recv, tot_send, tot_recv,
    send_sem, recv_sem, over_send, over_recv, load_sem,
):
    atoms_dev = chips * CORES
    capacity, features = slots.shape[1], slots.shape[2]
    share = features // chips
    atom_local = codes.shape[2]
    atoms_total = atom_local * atoms_dev
    span = half.shape[1]
    rows_core = PARTS * span
    lipschitz = 4.0 * (1.0 + math.sqrt(atoms_total / features)) ** 2
    g = lax.axis_index("dp")
    a = lax.axis_index("atom")
    z, k = a // CORES, a % CORES
    other = 1 - k
    sib = a + 1 - 2 * k
    mine_lanes = pl.ds(pl.multiple_of(k * atom_local, atom_local), atom_local)
    other_lanes = pl.ds(pl.multiple_of(other * atom_local, atom_local), atom_local)
    home = z == g
    started = []
    emptied = []

    def send(src, dst, device):
        i = len(started)
        copy = pltpu.make_async_remote_copy(
            src_ref=src, dst_ref=dst, send_sem=send_sem.at[i], recv_sem=recv_sem.at[i],
            device_id=device, device_id_type=MESH,
        )
        copy.start()
        started.append(copy)
        return copy

    def chip_of(mask):
        return flip(z, mask, chips)

    masks = list(range(chips - 1, 0, -1))

    load_slots = pltpu.make_async_copy(slots_hbm, slots.at[k], load_sem.at[0])
    load_slots.start()
    load_dict = pltpu.make_async_copy(dict_hbm, dic.at[k], load_sem.at[1])
    load_dict.start()

    barrier = pltpu.get_barrier_semaphore()
    for r in range(1, atoms_dev):
        pl.semaphore_signal(barrier, inc=1, device_id=(g, (a + r) % atoms_dev), device_id_type=MESH)
    for q in range(1, groups):
        pl.semaphore_signal(barrier, inc=1, device_id=((g + q) % groups, a), device_id_type=MESH)
        pl.semaphore_signal(
            barrier, inc=1, device_id=((g + q) % groups, g * CORES + k), device_id_type=MESH
        )

    @pl.when(jnp.logical_not(home))
    def _():
        pl.semaphore_signal(barrier, inc=1, device_id=(g, g * CORES + k), device_id_type=MESH)

    load_slots.wait()
    pl.semaphore_wait(barrier, atoms_dev - 1 + groups - 1 + chips - jnp.where(home, 1, 0))

    swap = send(slots.at[k], slots.at[k], (g, sib))
    picks = []
    slot = lax.broadcasted_iota(jnp.int32, (span, capacity), 1)
    row = lax.broadcasted_iota(jnp.int32, (span, capacity), 0) + k * rows_core
    for j in range(CORES):
        source = z * CORES + j
        start = jnp.int32(0)
        for i in range(atoms_dev):
            start = start + jnp.where(i < source, counts_ref[i], 0)
        count = counts_ref[source]
        for h in range(PARTS):
            hit = jnp.logical_and(row + h * span - start == slot, slot < count)
            picks.append(jnp.where(hit, -1.0, 0.0).astype(BF16))
    swap.wait_recv()
    load_dict.wait()
    share_dict = send(dic.at[k], dic.at[k], (g, sib))

    contributed = []
    for h in range(PARTS):
        part = jnp.dot(picks[h], slots[0], preferred_element_type=F32)
        part = part + jnp.dot(picks[PARTS + h], slots[1], preferred_element_type=F32)
        for c in range(chips):
            con_send[h, c] = part[:, c * share:(c + 1) * share].astype(BF16)
        if h:
            for c in contributed[h - 1]:
                c.wait_send()
                emptied.append(id(c))
        contributed.append([
            send(con_send.at[h, chip_of(x)], con_recv.at[h, x - 1], (g, chip_of(x) * CORES + k))
            for x in masks
        ])

    block = min(256, atom_local)
    unit = jnp.where(
        lax.broadcasted_iota(jnp.int32, (block, block), 0) == lax.broadcasted_iota(jnp.int32, (block, block), 1),
        1.0, 0.0,
    ).astype(BF16)

    def turn(j):
        for c in range(chips):
            for i in range(atom_local // block):
                rows = pl.ds(pl.multiple_of(j * atom_local + i * block, block), block)
                part = lax.dot_general(
                    unit, dic[j, c, :, i * block:(i + 1) * block], (((1,), (1,)), ((), ())),
                    preferred_element_type=F32,
                )
                dic_t[c, rows, :] = part.astype(BF16)

    def gather(t, h):
        return [
            send(gath.at[t, h, z], gath.at[t, h, z], (g, chip_of(x) * CORES + k)) for x in masks
        ]

    turn(k)
    gathers = []
    for h in range(PARTS):
        total = con_send[h, z].astype(F32)
        for c in contributed[h]:
            c.wait_recv()
        for x in masks:
            total = total + con_recv[h, x - 1].astype(F32)
        gath[0, h, z] = total.astype(BF16)
        gathers.append(gather(0, h))
    square_d = jnp.zeros((1, atom_local), F32)
    for c in range(chips):
        wide = dic[k, c].astype(F32)
        square_d = square_d + jnp.sum(wide * wide, axis=0, keepdims=True)
    share_dict.wait_recv()
    turn(other)

    tile = min(512, atom_local)

    def code(t, h, waits):
        rows = slice(h * span, (h + 1) * span)
        pairs = chips // 2

        def pair_of(i):
            return (z // 2 + i) % pairs

        def patches_of(i):
            block = gath[t, h, pl.ds(2 * pair_of(i), 2)]
            return jnp.concatenate([block[0], block[1]], axis=1)

        def product(i, x, j, cols):
            d = dic[j, pl.ds(2 * pair_of(i), 2), :, cols].reshape(2 * share, tile)
            return jnp.dot(x, d, preferred_element_type=F32)

        spots = [(j, i) for j in range(CORES) for i in range(atom_local // tile)]
        waits[-1].wait_recv()
        x = patches_of(0)
        for j, i in spots:
            cols = slice(i * tile, (i + 1) * tile)
            prod = product(0, x, j, cols)
            codes[j, rows, cols] = -prod if t == 0 else codes[j, rows, cols] - prod
        for c in waits[:-1]:
            c.wait_recv()
        xs = [patches_of(p) for p in range(1, pairs)]
        for j, i in spots:
            cols = slice(i * tile, (i + 1) * tile)
            new = codes[j, rows, cols]
            for p in range(1, pairs):
                new = new - product(p, xs[p - 1], j, cols)
            new = shrink(new)
            codes[j, rows, cols] = new
            half[h, :, j * atom_local + i * tile:j * atom_local + (i + 1) * tile] = new.astype(BF16)

    def known(history, t, h, slot):
        if t == 1:
            return 2.0 * history[0, h, slot]
        return 2.0 * history[t - 1, h, slot] - history[t - 2, h, slot]

    def recon_start(t, h):
        arrivals = []
        for x in masks:
            zz = chip_of(x)
            s = x - 1
            both = jnp.dot(half[h], dic_t[zz], preferred_element_type=F32)
            rows = span
            if t == 0:
                base = gath[0, h, zz].astype(F32)
                fit = jnp.sum(jnp.sum(both * base, axis=0, keepdims=True), axis=1, keepdims=True)
                norm = jnp.sum(jnp.sum(base * base, axis=0, keepdims=True), axis=1, keepdims=True)
                fit = (fit / (norm + 1e-30)).astype(LINK)
                z_send[t, h, s, span:] = jnp.broadcast_to(fit, (16, share))
                guess = fit.astype(F32) * base
                rows = span + 16
            else:
                guess = known(sent_sum, t, h, s)
            step = (both - guess).astype(LINK)
            z_send[t, h, s, :span] = step
            arrivals.append(
                (s, send(z_send.at[t, h, s, pl.ds(0, rows)], z_recv.at[t, h, s, pl.ds(0, rows)], (g, zz * CORES + k)))
            )
            if t < ITERS - 1:
                sent_sum[t, h, s] = guess + step.astype(F32)
        own_part[h] = jnp.dot(half[h], dic_t[z], preferred_element_type=F32)
        return arrivals

    def recon_end(t, h, arrivals):
        mine = own_part[h]
        negative = gath[0, h, z].astype(F32)
        for s, c in reversed(arrivals):
            c.wait_recv()
            if t == 0:
                guess = z_recv[t, h, s, span:span + 1].astype(F32) * negative
            else:
                guess = known(recv_sum, t, h, s)
            value = guess + z_recv[t, h, s, :span].astype(F32)
            if t < ITERS - 1:
                recv_sum[t, h, s] = value
            mine = mine + value
        return (mine / lipschitz + negative).astype(BF16)

    square = groups == 4
    near = [g // 2 * 2 + 1 - g % 2, (g + 2) % 4]
    half_moves, relayed, to_sib, locals_ = {}, {}, [], []

    def half_start(h):
        keep = pltpu.make_async_copy(half.at[h, :, mine_lanes], half_all.at[h, g, k], load_sem.at[2 + h])
        keep.start()
        locals_.append(keep)
        rows = pl.ds(pl.multiple_of(k * rows_core + h * span, span), span)
        keep = pltpu.make_async_copy(
            codes.at[k, pl.ds(h * span, span)], codes_out.at[rows], load_sem.at[2 + PARTS + h]
        )
        keep.start()
        locals_.append(keep)
        peers = near if square else [(g + q) % groups for q in range(1, groups)]
        for first in (True, False):
            for i, q in enumerate(peers):
                p = 1 - i % 2 if first else i % 2
                lanes, core = ((mine_lanes, a), (other_lanes, sib))[p]
                half_moves.setdefault((h, i), {})[p] = send(
                    half.at[h, :, lanes], half_all.at[h, g, k], (q, core)
                )
        to_sib.append(send(half.at[h, :, other_lanes], half_all.at[h, g, k], (g, sib)))

    def codes_start(h):
        rows = pl.ds(pl.multiple_of(k * rows_core + h * span, span), span)
        to_sib.append(send(codes.at[other, pl.ds(h * span, span)], codes_out.at[rows], (g, sib)))

    def relay(h):
        relayed[h] = []
        for p in range(2):
            half_moves[h, 1 - p][p].wait_recv()
            piece = half_all.at[h, near[1 - p], k if p == 0 else other]
            relayed[h].append(send(piece, piece, (near[p], a)))

    def half_end(h):
        if square:
            for p in range(2):
                half_moves[h, p][p].wait_recv()
                relayed[h][p].wait_recv()
        else:
            for q in range(1, groups):
                for c in half_moves[h, q - 1].values():
                    c.wait_recv()

    def over(h, r):
        zz = (z + r) % chips
        return pltpu.make_async_remote_copy(
            src_ref=resid.at[h], dst_ref=res_all.at[h, g, k], send_sem=over_send.at[h, r],
            recv_sem=over_recv.at[h, g], device_id=(z, zz * CORES + k), device_id_type=MESH,
        )

    def over_arrival(h, q):
        return pltpu.make_async_remote_copy(
            src_ref=resid.at[h], dst_ref=res_all.at[h, q, k], send_sem=over_send.at[h, 0],
            recv_sem=over_recv.at[h, q], device_id=(g, sib), device_id_type=MESH,
        )

    def over_start(h, value):
        resid[h] = value
        for r in range(1, chips):
            over(h, r).start()

        @pl.when(jnp.logical_not(home))
        def _():
            over(h, 0).start()

        @pl.when(home)
        def _():
            res_all[h, g, k] = value

    def over_end(h):
        for p in range(groups):
            q = (g + p) % groups
            if p:
                over_arrival(h, q).wait_recv()
            else:
                @pl.when(jnp.logical_not(home))
                def _():
                    over_arrival(h, q).wait_recv()
            to_sib.append(send(res_all.at[h, q, k], res_all.at[h, q, k], (g, sib)))

    for t in range(ITERS):
        last = t == ITERS - 1
        arrivals = []
        for h in range(PARTS):
            code(t, h, gathers[h])
            if last:
                half_start(h)
            arrivals.append(recon_start(t, h))
        gathers = []
        for h in range(PARTS):
            value = recon_end(t, h, arrivals[h])
            if last:
                over_start(h, value)
                if square:
                    relay(h)
                codes_start(h)
            else:
                gath[t + 1, h, z] = value
                gathers.append(gather(t + 1, h))

    done = 0
    cols_tile = min(256, atom_local)
    depth = groups * CORES * span
    for h in range(PARTS):
        half_end(h)
        over_end(h)
        for c in to_sib[done:]:
            c.wait_recv()
        done = len(to_sib)
        if h == 0:
            for c in locals_:
                c.wait()
        left = res_all[h].reshape(depth, share)
        for i in range(atom_local // cols_tile):
            cols = slice(i * cols_tile, (i + 1) * cols_tile)
            right = half_all[h, :, :, :, cols].reshape(depth, cols_tile)
            prod = lax.dot_general(left, right, (((0,), (0,)), ((), ())), preferred_element_type=F32)
            if h > 0:
                prod = grad[:, cols] + prod
            grad[:, cols] = prod
            if h == PARTS - 1:
                d = dic[k, g, :, cols].astype(F32)
                col_send[0:1, cols] = jnp.sum(d * prod, axis=0, keepdims=True)
                col_send[1:2, cols] = jnp.sum(prod * prod, axis=0, keepdims=True)

    total = jnp.sum(col_send[1:2], axis=1, keepdims=True)
    tot_send[...] = jnp.broadcast_to(total, tot_send.shape)
    moves = [send(col_send, col_recv.at[q - 1], ((g + q) % groups, a)) for q in range(1, groups)]
    everyone = [(q, r) for q in range(groups) for r in range(atoms_dev) if q or r]
    everyone.sort(key=lambda p: abs(p[1] - atoms_dev // 2))
    totals = [
        send(tot_send, tot_recv.at[i], ((g + q) % groups, (a + r) % atoms_dev))
        for i, (q, r) in enumerate(everyone)
    ]
    column = col_send[...]
    for q in range(1, groups):
        moves[q - 1].wait_recv()
        column = column + col_recv[q - 1]
    cross, square_g = column[0:1], column[1:2]
    for c in totals:
        c.wait_recv()
    line = tot_send[...] + jnp.sum(tot_recv[...], axis=0)
    scale = (0.5 * math.sqrt(atoms_total)) / jnp.sqrt(line[0:1, 0:1])
    norm = square_d + scale * (scale * square_g - 2.0 * cross)
    norm = jnp.where(scale == 0.0, square_d, jnp.maximum(norm, 0.0))
    inverse = 1.0 / jnp.sqrt(norm + 1e-06)
    own_rows = dic[k, g].astype(F32)
    newd_ref[...] = (own_rows - scale * grad[...]) * inverse
    for c in started:
        if id(c) not in emptied:
            c.wait_send()
    for h in range(PARTS):
        for r in range(1, chips):
            over(h, r).wait_send()

        @pl.when(jnp.logical_not(home))
        def _():
            over(h, 0).wait_send()


def finish(codes_ref, newd_ref, codes_out, newd_out, sem):
    copies = [
        pltpu.make_async_copy(codes_ref, codes_out, sem.at[0]),
        pltpu.make_async_copy(newd_ref, newd_out, sem.at[1]),
    ]
    for c in copies:
        c.start()
    for c in copies:
        c.wait()


def local(groups, chips, patch_slots, slot_counts, dictionary):
    atoms_dev = chips * CORES
    slots = patch_slots[0]
    capacity, features = slots.shape
    share = features // chips
    atom_local = dictionary.shape[1]
    blocks = dictionary.reshape(chips, share, atom_local)
    span = B // CORES // PARTS
    copies = (
        2 + 2 * ITERS * PARTS * (chips - 1) + PARTS * (2 * (groups - 1) + groups + 4)
        + (chips - 1) * PARTS + (groups - 1) + (groups * atoms_dev - 1)
    )
    codes, newd = pl.pallas_call(
        functools.partial(kernel, groups, chips),
        out_shape=(
            pltpu.VMEM((B, atom_local), F32),
            pltpu.VMEM((share, atom_local), F32),
        ),
        in_specs=[
            pl.BlockSpec(memory_space=pltpu.SMEM),
            pl.BlockSpec(memory_space=pl.ANY),
            pl.BlockSpec(memory_space=pl.ANY),
        ],
        out_specs=(pl.BlockSpec(memory_space=pltpu.VMEM), pl.BlockSpec(memory_space=pltpu.VMEM)),
        scratch_shapes=[
            pltpu.VMEM((CORES, capacity, features), BF16),
            pltpu.VMEM((CORES, chips, share, atom_local), BF16),
            pltpu.VMEM((chips, CORES * atom_local, share), BF16),
            pltpu.VMEM((PARTS, chips, span, share), BF16),
            pltpu.VMEM((PARTS, chips - 1, span, share), BF16),
            pltpu.VMEM((ITERS, PARTS, chips, span, share), BF16),
            pltpu.VMEM((CORES, PARTS * span, atom_local), F32),
            pltpu.VMEM((PARTS, span, CORES * atom_local), BF16),
            pltpu.VMEM((PARTS, span, share), F32),
            pltpu.VMEM((ITERS, PARTS, chips - 1, span + 16, share), LINK),
            pltpu.VMEM((ITERS, PARTS, chips - 1, span + 16, share), LINK),
            pltpu.VMEM((ITERS - 1, PARTS, chips - 1, span, share), F32),
            pltpu.VMEM((ITERS - 1, PARTS, chips - 1, span, share), F32),
            pltpu.VMEM((PARTS, span, share), BF16),
            pltpu.VMEM((PARTS, groups, CORES, span, atom_local), BF16),
            pltpu.VMEM((PARTS, groups, CORES, span, share), BF16),
            pltpu.VMEM((share, atom_local), F32),
            pltpu.VMEM((2, atom_local), F32),
            pltpu.VMEM((groups - 1, 2, atom_local), F32),
            pltpu.VMEM((1, 128), F32),
            pltpu.VMEM((groups * atoms_dev - 1, 1, 128), F32),
            pltpu.SemaphoreType.DMA((copies,)),
            pltpu.SemaphoreType.DMA((copies,)),
            pltpu.SemaphoreType.DMA((PARTS, chips)),
            pltpu.SemaphoreType.DMA((PARTS, groups)),
            pltpu.SemaphoreType.DMA((2 + 2 * PARTS,)),
        ],
        compiler_params=pltpu.CompilerParams(
            collective_id=0, has_side_effects=True, vmem_limit_bytes=61 * 1024 * 1024 + 786432
        ),
    )(slot_counts[0], slots, blocks)
    codes, newd = pl.pallas_call(
        finish,
        out_shape=(
            jax.ShapeDtypeStruct((B, atom_local), F32),
            jax.ShapeDtypeStruct((share, atom_local), F32),
        ),
        in_specs=[pl.BlockSpec(memory_space=pl.ANY)] * 2,
        out_specs=(pl.BlockSpec(memory_space=pl.ANY),) * 2,
        scratch_shapes=[pltpu.SemaphoreType.DMA((2,))],
        compiler_params=pltpu.CompilerParams(vmem_limit_bytes=8 * 1024 * 1024),
    )(codes, newd)
    return (codes[None], newd)


def solution(mesh):
    groups = mesh.shape["dp"]
    chips = mesh.shape["atom"] // CORES
    assert chips == groups and chips & (chips - 1) == 0
    placed = (P("dp", "atom", None), P("dp", None), P(None, "atom"))
    return jax.shard_map(
        functools.partial(local, groups, chips),
        mesh=mesh,
        in_specs=placed,
        out_specs=(P("dp", None, "atom"), P("dp", "atom")),
        check_vma=False,
    )
```

```python
import functools
import math

import jax
import jax.numpy as jnp
from jax import lax
from jax.experimental import pallas as pl
from jax.experimental.pallas import tpu as pltpu
from jax.sharding import PartitionSpec as P

B = 256
ITERS = 3
CORES = 2
PARTS = 2
LINK = jnp.bfloat16
MESH = pl.DeviceIdType.MESH
F32 = jnp.float32
BF16 = jnp.bfloat16


def shrink(values):
    return values - jnp.clip(values, -1.0, 1.0)


def flip(index, mask, size):
    bit = 1
    while bit < size:
        if mask & bit:
            index = index + bit * (1 - 2 * ((index // bit) % 2))
        bit *= 2
    return index


def kernel(
    groups, chips, counts_ref, slots_hbm, dict_hbm, codes_out, newd_ref,
    slots, dic, dic_t, con_send, con_recv, gath, codes, half, own_part, z_send, z_recv, sent_sum, recv_sum,
    resid, half_all, oth_gath, oth_codes, oth_half, res_all, grad, col_send, col_recv, tot_send, tot_recv,
    send_sem, recv_sem, over_send, over_recv, load_sem,
):
    atoms_dev = chips * CORES
    capacity, features = slots.shape[1], slots.shape[2]
    share = features // chips
    atom_local = codes.shape[2]
    atoms_total = atom_local * atoms_dev
    span = half.shape[1]
    rows_core = PARTS * span
    lipschitz = 4.0 * (1.0 + math.sqrt(atoms_total / features)) ** 2
    g = lax.axis_index("dp")
    a = lax.axis_index("atom")
    z, k = a // CORES, a % CORES
    other = 1 - k
    sib = a + 1 - 2 * k
    mine_lanes = pl.ds(pl.multiple_of(k * atom_local, atom_local), atom_local)
    other_lanes = pl.ds(pl.multiple_of(other * atom_local, atom_local), atom_local)
    home = z == g
    near_x, near_y = g // 2 * 2 + 1 - g % 2, (g + 2) % 4
    started = []
    emptied = []

    def send(src, dst, device):
        i = len(started)
        copy = pltpu.make_async_remote_copy(
            src_ref=src, dst_ref=dst, send_sem=send_sem.at[i], recv_sem=recv_sem.at[i],
            device_id=device, device_id_type=MESH,
        )
        copy.start()
        started.append(copy)
        return copy

    def chip_of(mask):
        return flip(z, mask, chips)

    masks = list(range(chips - 1, 0, -1))

    load_slots = pltpu.make_async_copy(slots_hbm, slots.at[k], load_sem.at[0])
    load_slots.start()
    load_dict = pltpu.make_async_copy(dict_hbm, dic.at[k], load_sem.at[1])
    load_dict.start()

    barrier = pltpu.get_barrier_semaphore()
    for r in range(1, atoms_dev):
        pl.semaphore_signal(barrier, inc=1, device_id=(g, (a + r) % atoms_dev), device_id_type=MESH)
    for q in range(1, groups):
        pl.semaphore_signal(barrier, inc=1, device_id=((g + q) % groups, a), device_id_type=MESH)
        pl.semaphore_signal(
            barrier, inc=1, device_id=((g + q) % groups, g * CORES + k), device_id_type=MESH
        )

    @pl.when(jnp.logical_not(home))
    def _():
        pl.semaphore_signal(barrier, inc=1, device_id=(g, g * CORES + k), device_id_type=MESH)

    load_slots.wait()
    pl.semaphore_wait(barrier, atoms_dev - 1 + groups - 1 + chips - jnp.where(home, 1, 0))

    swap = send(slots.at[k], slots.at[k], (g, sib))
    picks = []
    slot = lax.broadcasted_iota(jnp.int32, (span, capacity), 1)
    row = lax.broadcasted_iota(jnp.int32, (span, capacity), 0) + k * rows_core
    for j in range(CORES):
        source = z * CORES + j
        start = jnp.int32(0)
        for i in range(atoms_dev):
            start = start + jnp.where(i < source, counts_ref[i], 0)
        count = counts_ref[source]
        for h in range(PARTS):
            hit = jnp.logical_and(row + h * span - start == slot, slot < count)
            picks.append(jnp.where(hit, -1.0, 0.0).astype(BF16))
    swap.wait_recv()
    load_dict.wait()
    share_dict = send(dic.at[k], dic.at[k], (g, sib))

    contributed = []
    for h in range(PARTS):
        part = jnp.dot(picks[h], slots[0], preferred_element_type=F32)
        part = part + jnp.dot(picks[PARTS + h], slots[1], preferred_element_type=F32)
        for c in range(chips):
            con_send[h, c] = part[:, c * share:(c + 1) * share].astype(BF16)
        if h:
            for c in contributed[h - 1]:
                c.wait_send()
                emptied.append(id(c))
        contributed.append([
            send(con_send.at[h, chip_of(x)], con_recv.at[h, x - 1], (g, chip_of(x) * CORES + k))
            for x in masks
        ])

    block = min(256, atom_local)
    unit = jnp.where(
        lax.broadcasted_iota(jnp.int32, (block, block), 0) == lax.broadcasted_iota(jnp.int32, (block, block), 1),
        1.0, 0.0,
    ).astype(BF16)

    def turn(j):
        for c in range(chips):
            for i in range(atom_local // block):
                rows = pl.ds(pl.multiple_of(j * atom_local + i * block, block), block)
                part = lax.dot_general(
                    unit, dic[j, c, :, i * block:(i + 1) * block], (((1,), (1,)), ((), ())),
                    preferred_element_type=F32,
                )
                dic_t[c, rows, :] = part.astype(BF16)

    def gather(t, h):
        return [
            send(gath.at[t, h, z], gath.at[t, h, z], (g, chip_of(x) * CORES + k)) for x in masks
        ]

    turn(k)
    gathers = []
    for h in range(PARTS):
        total = con_send[h, z].astype(F32)
        for c in contributed[h]:
            c.wait_recv()
        for x in masks:
            total = total + con_recv[h, x - 1].astype(F32)
        gath[0, h, z] = total.astype(BF16)
        gathers.append(gather(0, h))
    square_d = jnp.zeros((1, atom_local), F32)
    for c in range(chips):
        wide = dic[k, c].astype(F32)
        square_d = square_d + jnp.sum(wide * wide, axis=0, keepdims=True)
    share_dict.wait_recv()
    turn(other)

    tile = min(512, atom_local)

    def code(t, h, waits):
        rows = slice(h * span, (h + 1) * span)
        pairs = chips // 2

        def pair_of(i):
            return (z // 2 + i) % pairs

        def patches_of(i):
            block = gath[t, h, pl.ds(2 * pair_of(i), 2)]
            return jnp.concatenate([block[0], block[1]], axis=1)

        def product(i, x, j, cols):
            d = dic[j, pl.ds(2 * pair_of(i), 2), :, cols].reshape(2 * share, tile)
            return jnp.dot(x, d, preferred_element_type=F32)

        spots = [(j, i) for j in range(CORES) for i in range(atom_local // tile)]
        waits[-1].wait_recv()
        x = patches_of(0)
        for j, i in spots:
            cols = slice(i * tile, (i + 1) * tile)
            prod = product(0, x, j, cols)
            codes[j, rows, cols] = -prod if t == 0 else codes[j, rows, cols] - prod
        for c in waits[:-1]:
            c.wait_recv()
        if square:
            spread(t, h)
        xs = [patches_of(p) for p in range(1, pairs)]
        for j, i in spots:
            cols = slice(i * tile, (i + 1) * tile)
            new = codes[j, rows, cols]
            for p in range(1, pairs):
                new = new - product(p, xs[p - 1], j, cols)
            new = shrink(new)
            codes[j, rows, cols] = new
            half[h, :, j * atom_local + i * tile:j * atom_local + (i + 1) * tile] = new.astype(BF16)

    def known(history, t, h, slot):
        if t == 1:
            return 2.0 * history[0, h, slot]
        return 2.0 * history[t - 1, h, slot] - history[t - 2, h, slot]

    def recon_start(t, h):
        arrivals = []
        for x in masks:
            zz = chip_of(x)
            s = x - 1
            both = jnp.dot(half[h], dic_t[zz], preferred_element_type=F32)
            rows = span
            if t == 0:
                base = gath[0, h, zz].astype(F32)
                fit = jnp.sum(jnp.sum(both * base, axis=0, keepdims=True), axis=1, keepdims=True)
                norm = jnp.sum(jnp.sum(base * base, axis=0, keepdims=True), axis=1, keepdims=True)
                fit = (fit / (norm + 1e-30)).astype(LINK)
                z_send[t, h, s, span:] = jnp.broadcast_to(fit, (16, share))
                guess = fit.astype(F32) * base
                rows = span + 16
            else:
                guess = known(sent_sum, t, h, s)
            step = (both - guess).astype(LINK)
            z_send[t, h, s, :span] = step
            arrivals.append(
                (s, send(z_send.at[t, h, s, pl.ds(0, rows)], z_recv.at[t, h, s, pl.ds(0, rows)], (g, zz * CORES + k)))
            )
            if t < ITERS - 1:
                sent_sum[t, h, s] = guess + step.astype(F32)
        own_part[h] = jnp.dot(half[h], dic_t[z], preferred_element_type=F32)
        return arrivals

    def recon_end(t, h, arrivals):
        mine = own_part[h]
        negative = gath[0, h, z].astype(F32)
        for s, c in reversed(arrivals):
            c.wait_recv()
            if t == 0:
                guess = z_recv[t, h, s, span:span + 1].astype(F32) * negative
            else:
                guess = known(recv_sum, t, h, s)
            value = guess + z_recv[t, h, s, :span].astype(F32)
            if t < ITERS - 1:
                recv_sum[t, h, s] = value
            mine = mine + value
        return (mine / lipschitz + negative).astype(BF16)

    square = groups == 4
    slots_of = [near_x, near_y, groups - 1 - g] if square else []
    near = [near_x, near_y]
    half_moves, relayed, to_sib, locals_ = {}, {}, [], []

    def half_start(h):
        keep = pltpu.make_async_copy(half.at[h, :, mine_lanes], half_all.at[h, g, k], load_sem.at[2 + h])
        keep.start()
        locals_.append(keep)
        rows = pl.ds(pl.multiple_of(k * rows_core + h * span, span), span)
        keep = pltpu.make_async_copy(
            codes.at[k, pl.ds(h * span, span)], codes_out.at[rows], load_sem.at[2 + PARTS + h]
        )
        keep.start()
        locals_.append(keep)
        for q in ([] if square else range(1, groups)):
            peer = (g + q) % groups
            half_moves[h, q] = (
                send(half.at[h, :, mine_lanes], half_all.at[h, g, k], (peer, a)),
                send(half.at[h, :, other_lanes], half_all.at[h, g, k], (peer, sib)),
            )
        to_sib.append(send(half.at[h, :, other_lanes], half_all.at[h, g, k], (g, sib)))

    def codes_start(h):
        rows = pl.ds(pl.multiple_of(k * rows_core + h * span, span), span)
        to_sib.append(send(codes.at[other, pl.ds(h * span, span)], codes_out.at[rows], (g, sib)))

    def spread(t, h):
        half_moves[t, h] = [send(gath.at[t, h], oth_gath.at[t, h, i], (near[i], a)) for i in range(2)]

    def relay(t, h):
        relayed[t, h] = []
        for p in range(2):
            half_moves[t, h][1 - p].wait_recv()
            blocks = pl.ds(p * (chips // 2), chips // 2)
            relayed[t, h].append(
                send(oth_gath.at[t, h, 1 - p, blocks], oth_gath.at[t, h, 2, blocks], (near[p], a))
            )

    def others(t, h):
        last = t == ITERS - 1
        for c in relayed[t, h]:
            c.wait_recv()
        x = jnp.concatenate(
            [
                jnp.concatenate([oth_gath[t, h, i, c] for c in range(chips)], axis=1)
                for i in range(groups - 1)
            ],
            axis=0,
        )
        for j in (other, k):
            for i in range(atom_local // tile):
                cols = slice(i * tile, (i + 1) * tile)
                d = dic[j, :, :, cols].reshape(features, tile)
                prod = jnp.dot(x, d, preferred_element_type=F32)
                new = shrink(-prod if t == 0 else oth_codes[h, j, :, cols] - prod)
                if not last:
                    oth_codes[h, j, :, cols] = new
                    continue
                new = new.astype(BF16)
                for q in range(groups - 1):
                    rows = new[q * span:(q + 1) * span]
                    if j is k:
                        half_all[h, slots_of[q], k, :, cols] = rows
                    else:
                        oth_half[h, q, :, cols] = rows
            if last and j is not k:
                for q in range(groups - 1):
                    to_sib.append(send(oth_half.at[h, q], half_all.at[h, slots_of[q], k], (g, sib)))

    def half_end(h):
        if square:
            others(ITERS - 1, h)
        else:
            for q in range(1, groups):
                for c in half_moves[h, q]:
                    c.wait_recv()

    def over(h, r):
        zz = (z + r) % chips
        return pltpu.make_async_remote_copy(
            src_ref=resid.at[h], dst_ref=res_all.at[h, g, k], send_sem=over_send.at[h, r],
            recv_sem=over_recv.at[h, g], device_id=(z, zz * CORES + k), device_id_type=MESH,
        )

    def over_arrival(h, q):
        return pltpu.make_async_remote_copy(
            src_ref=resid.at[h], dst_ref=res_all.at[h, q, k], send_sem=over_send.at[h, 0],
            recv_sem=over_recv.at[h, q], device_id=(g, sib), device_id_type=MESH,
        )

    def over_start(h, value):
        resid[h] = value
        for r in range(1, chips):
            over(h, r).start()

        @pl.when(jnp.logical_not(home))
        def _():
            over(h, 0).start()

        @pl.when(home)
        def _():
            res_all[h, g, k] = value

    def over_end(h):
        for p in range(groups):
            q = (g + p) % groups
            if p:
                over_arrival(h, q).wait_recv()
            else:
                @pl.when(jnp.logical_not(home))
                def _():
                    over_arrival(h, q).wait_recv()
            to_sib.append(send(res_all.at[h, q, k], res_all.at[h, q, k], (g, sib)))

    for t in range(ITERS):
        last = t == ITERS - 1
        arrivals = []
        for h in range(PARTS):
            code(t, h, gathers[h])
            if last:
                half_start(h)
            arrivals.append(recon_start(t, h))
        gathers = []
        for h in range(PARTS):
            value = recon_end(t, h, arrivals[h])
            if last:
                over_start(h, value)
                codes_start(h)
                if square and h < PARTS - 1:
                    relay(t, h)
            else:
                gath[t + 1, h, z] = value
                gathers.append(gather(t + 1, h))
        if square:
            for h in range(PARTS):
                if t:
                    others(t - 1, h)
                if last and h == 0:
                    relay(t, PARTS - 1)
            for h in range(PARTS):
                if not last:
                    relay(t, h)

    done = 0
    cols_tile = min(256, atom_local)
    depth = groups * CORES * span
    for h in range(PARTS):
        half_end(h)
        over_end(h)
        for c in to_sib[done:]:
            c.wait_recv()
        done = len(to_sib)
        if h == 0:
            for c in locals_:
                c.wait()
        left = res_all[h].reshape(depth, share)
        for i in range(atom_local // cols_tile):
            cols = slice(i * cols_tile, (i + 1) * cols_tile)
            right = half_all[h, :, :, :, cols].reshape(depth, cols_tile)
            prod = lax.dot_general(left, right, (((0,), (0,)), ((), ())), preferred_element_type=F32)
            if h > 0:
                prod = grad[:, cols] + prod
            grad[:, cols] = prod
            if h == PARTS - 1:
                d = dic[k, g, :, cols].astype(F32)
                col_send[0:1, cols] = jnp.sum(d * prod, axis=0, keepdims=True)
                col_send[1:2, cols] = jnp.sum(prod * prod, axis=0, keepdims=True)

    total = jnp.sum(col_send[1:2], axis=1, keepdims=True)
    tot_send[...] = jnp.broadcast_to(total, tot_send.shape)
    moves = [send(col_send, col_recv.at[q - 1], ((g + q) % groups, a)) for q in range(1, groups)]
    everyone = [(q, r) for q in range(groups) for r in range(atoms_dev) if q or r]
    everyone.sort(key=lambda p: abs(p[1] - atoms_dev // 2))
    totals = [
        send(tot_send, tot_recv.at[i], ((g + q) % groups, (a + r) % atoms_dev))
        for i, (q, r) in enumerate(everyone)
    ]
    column = col_send[...]
    for q in range(1, groups):
        moves[q - 1].wait_recv()
        column = column + col_recv[q - 1]
    cross, square_g = column[0:1], column[1:2]
    for c in totals:
        c.wait_recv()
    line = tot_send[...] + jnp.sum(tot_recv[...], axis=0)
    scale = (0.5 * math.sqrt(atoms_total)) / jnp.sqrt(line[0:1, 0:1])
    norm = square_d + scale * (scale * square_g - 2.0 * cross)
    norm = jnp.where(scale == 0.0, square_d, jnp.maximum(norm, 0.0))
    inverse = 1.0 / jnp.sqrt(norm + 1e-06)
    own_rows = dic[k, g].astype(F32)
    newd_ref[...] = (own_rows - scale * grad[...]) * inverse
    for c in started:
        if id(c) not in emptied:
            c.wait_send()
    for h in range(PARTS):
        for r in range(1, chips):
            over(h, r).wait_send()

        @pl.when(jnp.logical_not(home))
        def _():
            over(h, 0).wait_send()


def finish(codes_ref, newd_ref, codes_out, newd_out, sem):
    copies = [
        pltpu.make_async_copy(codes_ref, codes_out, sem.at[0]),
        pltpu.make_async_copy(newd_ref, newd_out, sem.at[1]),
    ]
    for c in copies:
        c.start()
    for c in copies:
        c.wait()


def local(groups, chips, patch_slots, slot_counts, dictionary):
    atoms_dev = chips * CORES
    slots = patch_slots[0]
    capacity, features = slots.shape
    share = features // chips
    atom_local = dictionary.shape[1]
    blocks = dictionary.reshape(chips, share, atom_local)
    span = B // CORES // PARTS
    if groups == 4:
        oth_gath = (ITERS, PARTS, groups - 1, chips, span, share)
        oth_codes = (PARTS, CORES, (groups - 1) * span, atom_local)
        oth_half = (PARTS, groups - 1, span, atom_local)
    else:
        oth_gath = oth_codes = oth_half = (8, 128)
    copies = (
        2 + 2 * ITERS * PARTS * (chips - 1) + PARTS * (3 * groups + 4 * ITERS + 4)
        + (chips - 1) * PARTS + (groups - 1) + (groups * atoms_dev - 1)
    )
    codes, newd = pl.pallas_call(
        functools.partial(kernel, groups, chips),
        out_shape=(
            pltpu.VMEM((B, atom_local), F32),
            pltpu.VMEM((share, atom_local), F32),
        ),
        in_specs=[
            pl.BlockSpec(memory_space=pltpu.SMEM),
            pl.BlockSpec(memory_space=pl.ANY),
            pl.BlockSpec(memory_space=pl.ANY),
        ],
        out_specs=(pl.BlockSpec(memory_space=pltpu.VMEM), pl.BlockSpec(memory_space=pltpu.VMEM)),
        scratch_shapes=[
            pltpu.VMEM((CORES, capacity, features), BF16),
            pltpu.VMEM((CORES, chips, share, atom_local), BF16),
            pltpu.VMEM((chips, CORES * atom_local, share), BF16),
            pltpu.VMEM((PARTS, chips, span, share), BF16),
            pltpu.VMEM((PARTS, chips - 1, span, share), BF16),
            pltpu.VMEM((ITERS, PARTS, chips, span, share), BF16),
            pltpu.VMEM((CORES, PARTS * span, atom_local), F32),
            pltpu.VMEM((PARTS, span, CORES * atom_local), BF16),
            pltpu.VMEM((PARTS, span, share), F32),
            pltpu.VMEM((ITERS, PARTS, chips - 1, span + 16, share), LINK),
            pltpu.VMEM((ITERS, PARTS, chips - 1, span + 16, share), LINK),
            pltpu.VMEM((ITERS - 1, PARTS, chips - 1, span, share), F32),
            pltpu.VMEM((ITERS - 1, PARTS, chips - 1, span, share), F32),
            pltpu.VMEM((PARTS, span, share), BF16),
            pltpu.VMEM((PARTS, groups, CORES, span, atom_local), BF16),
            pltpu.VMEM(oth_gath, BF16),
            pltpu.VMEM(oth_codes, F32),
            pltpu.VMEM(oth_half, BF16),
            pltpu.VMEM((PARTS, groups, CORES, span, share), BF16),
            pltpu.VMEM((share, atom_local), F32),
            pltpu.VMEM((2, atom_local), F32),
            pltpu.VMEM((groups - 1, 2, atom_local), F32),
            pltpu.VMEM((1, 128), F32),
            pltpu.VMEM((groups * atoms_dev - 1, 1, 128), F32),
            pltpu.SemaphoreType.DMA((copies,)),
            pltpu.SemaphoreType.DMA((copies,)),
            pltpu.SemaphoreType.DMA((PARTS, chips)),
            pltpu.SemaphoreType.DMA((PARTS, groups)),
            pltpu.SemaphoreType.DMA((2 + 2 * PARTS,)),
        ],
        compiler_params=pltpu.CompilerParams(
            collective_id=0, has_side_effects=True, vmem_limit_bytes=61 * 1024 * 1024 + 786432
        ),
    )(slot_counts[0], slots, blocks)
    codes, newd = pl.pallas_call(
        finish,
        out_shape=(
            jax.ShapeDtypeStruct((B, atom_local), F32),
            jax.ShapeDtypeStruct((share, atom_local), F32),
        ),
        in_specs=[pl.BlockSpec(memory_space=pl.ANY)] * 2,
        out_specs=(pl.BlockSpec(memory_space=pl.ANY),) * 2,
        scratch_shapes=[pltpu.SemaphoreType.DMA((2,))],
        compiler_params=pltpu.CompilerParams(vmem_limit_bytes=8 * 1024 * 1024),
    )(codes, newd)
    return (codes[None], newd)


def solution(mesh):
    groups = mesh.shape["dp"]
    chips = mesh.shape["atom"] // CORES
    assert chips == groups and chips & (chips - 1) == 0
    placed = (P("dp", "atom", None), P("dp", None), P(None, "atom"))
    return jax.shard_map(
        functools.partial(local, groups, chips),
        mesh=mesh,
        in_specs=placed,
        out_specs=(P("dp", None, "atom"), P("dp", "atom")),
        check_vma=False,
    )
```

```python
import functools
import math

import jax
import jax.numpy as jnp
from jax import lax
from jax.experimental import pallas as pl
from jax.experimental.pallas import tpu as pltpu
from jax.sharding import PartitionSpec as P

B = 256
ITERS = 3
CORES = 2
PARTS = 2
LINK = jnp.bfloat16
MESH = pl.DeviceIdType.MESH
F32 = jnp.float32
BF16 = jnp.bfloat16


def shrink(values):
    return values - jnp.clip(values, -1.0, 1.0)


def flip(index, mask, size):
    bit = 1
    while bit < size:
        if mask & bit:
            index = index + bit * (1 - 2 * ((index // bit) % 2))
        bit *= 2
    return index


def kernel(
    groups, chips, counts_ref, slots_hbm, dict_hbm, codes_out, newd_ref,
    slots, dic, dic_t, con_send, con_recv, gath, codes, half, own_part, z_send, z_recv, sent_sum, recv_sum,
    resid, half_all, oth_gath, oth_codes, oth_half, res_all, grad, col_send, col_recv, tot_send, tot_recv,
    send_sem, recv_sem, over_send, over_recv, load_sem,
):
    atoms_dev = chips * CORES
    capacity, features = slots.shape[1], slots.shape[2]
    share = features // chips
    atom_local = codes.shape[2]
    atoms_total = atom_local * atoms_dev
    span = half.shape[1]
    rows_core = PARTS * span
    lipschitz = 4.0 * (1.0 + math.sqrt(atoms_total / features)) ** 2
    g = lax.axis_index("dp")
    a = lax.axis_index("atom")
    z, k = a // CORES, a % CORES
    other = 1 - k
    sib = a + 1 - 2 * k
    mine_lanes = pl.ds(pl.multiple_of(k * atom_local, atom_local), atom_local)
    other_lanes = pl.ds(pl.multiple_of(other * atom_local, atom_local), atom_local)
    home = z == g
    near_x, near_y = g // 2 * 2 + 1 - g % 2, (g + 2) % 4
    started = []
    emptied = []

    def send(src, dst, device):
        i = len(started)
        copy = pltpu.make_async_remote_copy(
            src_ref=src, dst_ref=dst, send_sem=send_sem.at[i], recv_sem=recv_sem.at[i],
            device_id=device, device_id_type=MESH,
        )
        copy.start()
        started.append(copy)
        return copy

    def chip_of(mask):
        return flip(z, mask, chips)

    masks = list(range(chips - 1, 0, -1))

    load_slots = pltpu.make_async_copy(slots_hbm, slots.at[k], load_sem.at[0])
    load_slots.start()
    load_dict = pltpu.make_async_copy(dict_hbm, dic.at[k], load_sem.at[1])
    load_dict.start()

    barrier = pltpu.get_barrier_semaphore()
    for r in range(1, atoms_dev):
        pl.semaphore_signal(barrier, inc=1, device_id=(g, (a + r) % atoms_dev), device_id_type=MESH)
    for q in range(1, groups):
        pl.semaphore_signal(barrier, inc=1, device_id=((g + q) % groups, a), device_id_type=MESH)
        pl.semaphore_signal(
            barrier, inc=1, device_id=((g + q) % groups, g * CORES + k), device_id_type=MESH
        )

    @pl.when(jnp.logical_not(home))
    def _():
        pl.semaphore_signal(barrier, inc=1, device_id=(g, g * CORES + k), device_id_type=MESH)

    load_slots.wait()
    pl.semaphore_wait(barrier, atoms_dev - 1 + groups - 1 + chips - jnp.where(home, 1, 0))

    swap = send(slots.at[k], slots.at[k], (g, sib))
    picks = []
    slot = lax.broadcasted_iota(jnp.int32, (span, capacity), 1)
    row = lax.broadcasted_iota(jnp.int32, (span, capacity), 0) + k * rows_core
    for j in range(CORES):
        source = z * CORES + j
        start = jnp.int32(0)
        for i in range(atoms_dev):
            start = start + jnp.where(i < source, counts_ref[i], 0)
        count = counts_ref[source]
        for h in range(PARTS):
            hit = jnp.logical_and(row + h * span - start == slot, slot < count)
            picks.append(jnp.where(hit, -1.0, 0.0).astype(BF16))
    swap.wait_recv()
    load_dict.wait()
    share_dict = send(dic.at[k], dic.at[k], (g, sib))

    contributed = []
    for h in range(PARTS):
        part = jnp.dot(picks[h], slots[0], preferred_element_type=F32)
        part = part + jnp.dot(picks[PARTS + h], slots[1], preferred_element_type=F32)
        for c in range(chips):
            con_send[h, c] = part[:, c * share:(c + 1) * share].astype(BF16)
        if h:
            for c in contributed[h - 1]:
                c.wait_send()
                emptied.append(id(c))
        contributed.append([
            send(con_send.at[h, chip_of(x)], con_recv.at[h, x - 1], (g, chip_of(x) * CORES + k))
            for x in masks
        ])

    block = min(256, atom_local)
    unit = jnp.where(
        lax.broadcasted_iota(jnp.int32, (block, block), 0) == lax.broadcasted_iota(jnp.int32, (block, block), 1),
        1.0, 0.0,
    ).astype(BF16)

    def turn(j):
        for c in range(chips):
            for i in range(atom_local // block):
                rows = pl.ds(pl.multiple_of(j * atom_local + i * block, block), block)
                part = lax.dot_general(
                    unit, dic[j, c, :, i * block:(i + 1) * block], (((1,), (1,)), ((), ())),
                    preferred_element_type=F32,
                )
                dic_t[c, rows, :] = part.astype(BF16)

    def gather(t, h):
        return [
            send(gath.at[t, h, z], gath.at[t, h, z], (g, chip_of(x) * CORES + k)) for x in masks
        ]

    turn(k)
    gathers = []
    for h in range(PARTS):
        total = con_send[h, z].astype(F32)
        for c in contributed[h]:
            c.wait_recv()
        for x in masks:
            total = total + con_recv[h, x - 1].astype(F32)
        gath[0, h, z] = total.astype(BF16)
        gathers.append(gather(0, h))
    square_d = jnp.zeros((1, atom_local), F32)
    for c in range(chips):
        wide = dic[k, c].astype(F32)
        square_d = square_d + jnp.sum(wide * wide, axis=0, keepdims=True)
    share_dict.wait_recv()
    turn(other)

    tile = min(512, atom_local)

    def code(t, h, waits):
        rows = slice(h * span, (h + 1) * span)
        pairs = chips // 2

        def pair_of(i):
            return (z // 2 + i) % pairs

        def patches_of(i):
            block = gath[t, h, pl.ds(2 * pair_of(i), 2)]
            return jnp.concatenate([block[0], block[1]], axis=1)

        def product(i, x, j, cols):
            d = dic[j, pl.ds(2 * pair_of(i), 2), :, cols].reshape(2 * share, tile)
            return jnp.dot(x, d, preferred_element_type=F32)

        spots = [(j, i) for j in range(CORES) for i in range(atom_local // tile)]
        waits[-1].wait_recv()
        x = patches_of(0)
        for j, i in spots:
            cols = slice(i * tile, (i + 1) * tile)
            prod = product(0, x, j, cols)
            codes[j, rows, cols] = -prod if t == 0 else codes[j, rows, cols] - prod
        for c in waits[:-1]:
            c.wait_recv()
        if square:
            spread(t, h)
        xs = [patches_of(p) for p in range(1, pairs)]
        for j, i in spots:
            cols = slice(i * tile, (i + 1) * tile)
            new = codes[j, rows, cols]
            for p in range(1, pairs):
                new = new - product(p, xs[p - 1], j, cols)
            new = shrink(new)
            codes[j, rows, cols] = new
            half[h, :, j * atom_local + i * tile:j * atom_local + (i + 1) * tile] = new.astype(BF16)

    def known(history, t, h, slot):
        if t == 1:
            return 2.0 * history[0, h, slot]
        return 2.0 * history[t - 1, h, slot] - history[t - 2, h, slot]

    def recon_start(t, h):
        arrivals = []
        for x in masks:
            zz = chip_of(x)
            s = x - 1
            both = jnp.dot(half[h], dic_t[zz], preferred_element_type=F32)
            rows = span
            if t == 0:
                base = gath[0, h, zz].astype(F32)
                fit = jnp.sum(jnp.sum(both * base, axis=0, keepdims=True), axis=1, keepdims=True)
                norm = jnp.sum(jnp.sum(base * base, axis=0, keepdims=True), axis=1, keepdims=True)
                fit = (fit / (norm + 1e-30)).astype(LINK)
                z_send[t, h, s, span:] = jnp.broadcast_to(fit, (16, share))
                guess = fit.astype(F32) * base
                rows = span + 16
            else:
                guess = known(sent_sum, t, h, s)
            step = (both - guess).astype(LINK)
            z_send[t, h, s, :span] = step
            arrivals.append(
                (s, send(z_send.at[t, h, s, pl.ds(0, rows)], z_recv.at[t, h, s, pl.ds(0, rows)], (g, zz * CORES + k)))
            )
            if t < ITERS - 1:
                sent_sum[t, h, s] = guess + step.astype(F32)
        own_part[h] = jnp.dot(half[h], dic_t[z], preferred_element_type=F32)
        return arrivals

    def recon_end(t, h, arrivals):
        mine = own_part[h]
        negative = gath[0, h, z].astype(F32)
        for s, c in reversed(arrivals):
            c.wait_recv()
            if t == 0:
                guess = z_recv[t, h, s, span:span + 1].astype(F32) * negative
            else:
                guess = known(recv_sum, t, h, s)
            value = guess + z_recv[t, h, s, :span].astype(F32)
            if t < ITERS - 1:
                recv_sum[t, h, s] = value
            mine = mine + value
        return (mine / lipschitz + negative).astype(BF16)

    square = groups == 4
    slots_of = [near_x, near_y, groups - 1 - g] if square else []
    near = [near_x, near_y]
    half_moves, relayed, to_sib, locals_ = {}, {}, [], []

    def half_start(h):
        keep = pltpu.make_async_copy(half.at[h, :, mine_lanes], half_all.at[h, g, k], load_sem.at[2 + h])
        keep.start()
        locals_.append(keep)
        rows = pl.ds(pl.multiple_of(k * rows_core + h * span, span), span)
        keep = pltpu.make_async_copy(
            codes.at[k, pl.ds(h * span, span)], codes_out.at[rows], load_sem.at[2 + PARTS + h]
        )
        keep.start()
        locals_.append(keep)
        for q in ([] if square else range(1, groups)):
            peer = (g + q) % groups
            half_moves[h, q] = (
                send(half.at[h, :, mine_lanes], half_all.at[h, g, k], (peer, a)),
                send(half.at[h, :, other_lanes], half_all.at[h, g, k], (peer, sib)),
            )
        to_sib.append(send(half.at[h, :, other_lanes], half_all.at[h, g, k], (g, sib)))

    def codes_start(h):
        rows = pl.ds(pl.multiple_of(k * rows_core + h * span, span), span)
        to_sib.append(send(codes.at[other, pl.ds(h * span, span)], codes_out.at[rows], (g, sib)))

    def spread(t, h):
        half_moves[t, h] = [send(gath.at[t, h], oth_gath.at[t, h, i], (near[i], a)) for i in range(2)]

    def relay(t, h):
        relayed[t, h] = []
        for p in range(2):
            half_moves[t, h][1 - p].wait_recv()
            blocks = pl.ds(p * (chips // 2), chips // 2)
            relayed[t, h].append(
                send(oth_gath.at[t, h, 1 - p, blocks], oth_gath.at[t, h, 2, blocks], (near[p], a))
            )

    def others(t, h):
        last = t == ITERS - 1
        for c in relayed[t, h]:
            c.wait_recv()
        x = jnp.concatenate(
            [
                jnp.concatenate([oth_gath[t, h, i, c] for c in range(chips)], axis=1)
                for i in range(groups - 1)
            ],
            axis=0,
        )
        for j in (other, k):
            for i in range(atom_local // 256):
                cols = slice(i * 256, (i + 1) * 256)
                d = dic[j, :, :, cols].reshape(features, 256)
                prod = jnp.dot(x, d, preferred_element_type=F32)
                new = shrink(-prod if t == 0 else oth_codes[h, j, :, cols] - prod)
                if not last:
                    oth_codes[h, j, :, cols] = new
                    continue
                new = new.astype(BF16)
                for q in range(groups - 1):
                    rows = new[q * span:(q + 1) * span]
                    if j is k:
                        half_all[h, slots_of[q], k, :, cols] = rows
                    else:
                        oth_half[h, q, :, cols] = rows
            if last and j is not k:
                for q in range(groups - 1):
                    to_sib.append(send(oth_half.at[h, q], half_all.at[h, slots_of[q], k], (g, sib)))

    def half_end(h):
        if square:
            others(ITERS - 1, h)
        else:
            for q in range(1, groups):
                for c in half_moves[h, q]:
                    c.wait_recv()

    def over(h, r):
        zz = (z + r) % chips
        return pltpu.make_async_remote_copy(
            src_ref=resid.at[h], dst_ref=res_all.at[h, g, k], send_sem=over_send.at[h, r],
            recv_sem=over_recv.at[h, g], device_id=(z, zz * CORES + k), device_id_type=MESH,
        )

    def over_arrival(h, q):
        return pltpu.make_async_remote_copy(
            src_ref=resid.at[h], dst_ref=res_all.at[h, q, k], send_sem=over_send.at[h, 0],
            recv_sem=over_recv.at[h, q], device_id=(g, sib), device_id_type=MESH,
        )

    def over_start(h, value):
        resid[h] = value
        for r in range(1, chips):
            over(h, r).start()

        @pl.when(jnp.logical_not(home))
        def _():
            over(h, 0).start()

        @pl.when(home)
        def _():
            res_all[h, g, k] = value

    def over_end(h):
        for p in range(groups):
            q = (g + p) % groups
            if p:
                over_arrival(h, q).wait_recv()
            else:
                @pl.when(jnp.logical_not(home))
                def _():
                    over_arrival(h, q).wait_recv()
            to_sib.append(send(res_all.at[h, q, k], res_all.at[h, q, k], (g, sib)))

    for t in range(ITERS):
        last = t == ITERS - 1
        arrivals = []
        for h in range(PARTS):
            code(t, h, gathers[h])
            if last:
                half_start(h)
            arrivals.append(recon_start(t, h))
        gathers = []
        for h in range(PARTS):
            value = recon_end(t, h, arrivals[h])
            if last:
                over_start(h, value)
                codes_start(h)
                if square and h < PARTS - 1:
                    relay(t, h)
            else:
                gath[t + 1, h, z] = value
                gathers.append(gather(t + 1, h))
        if square:
            for h in range(PARTS):
                if t == 1 and h == 0:
                    relay(t, 0)
                if t:
                    others(t - 1, h)
                if last and h == 0:
                    relay(t, PARTS - 1)
            for h in range(PARTS):
                if not last and not (t == 1 and h == 0):
                    relay(t, h)

    done = 0
    cols_tile = min(256, atom_local)
    depth = groups * CORES * span
    for h in range(PARTS):
        half_end(h)
        over_end(h)
        for c in to_sib[done:]:
            c.wait_recv()
        done = len(to_sib)
        if h == 0:
            for c in locals_:
                c.wait()
        left = res_all[h].reshape(depth, share)
        for i in range(atom_local // cols_tile):
            cols = slice(i * cols_tile, (i + 1) * cols_tile)
            right = half_all[h, :, :, :, cols].reshape(depth, cols_tile)
            prod = lax.dot_general(left, right, (((0,), (0,)), ((), ())), preferred_element_type=F32)
            if h > 0:
                prod = grad[:, cols] + prod
            grad[:, cols] = prod
            if h == PARTS - 1:
                d = dic[k, g, :, cols].astype(F32)
                col_send[0:1, cols] = jnp.sum(d * prod, axis=0, keepdims=True)
                col_send[1:2, cols] = jnp.sum(prod * prod, axis=0, keepdims=True)

    total = jnp.sum(col_send[1:2], axis=1, keepdims=True)
    tot_send[...] = jnp.broadcast_to(total, tot_send.shape)
    moves = [send(col_send, col_recv.at[q - 1], ((g + q) % groups, a)) for q in range(1, groups)]
    everyone = [(q, r) for q in range(groups) for r in range(atoms_dev) if q or r]
    everyone.sort(key=lambda p: abs(p[1] - atoms_dev // 2))
    totals = [
        send(tot_send, tot_recv.at[i], ((g + q) % groups, (a + r) % atoms_dev))
        for i, (q, r) in enumerate(everyone)
    ]
    column = col_send[...]
    for q in range(1, groups):
        moves[q - 1].wait_recv()
        column = column + col_recv[q - 1]
    cross, square_g = column[0:1], column[1:2]
    for c in totals:
        c.wait_recv()
    line = tot_send[...] + jnp.sum(tot_recv[...], axis=0)
    scale = (0.5 * math.sqrt(atoms_total)) / jnp.sqrt(line[0:1, 0:1])
    norm = square_d + scale * (scale * square_g - 2.0 * cross)
    norm = jnp.where(scale == 0.0, square_d, jnp.maximum(norm, 0.0))
    inverse = 1.0 / jnp.sqrt(norm + 1e-06)
    own_rows = dic[k, g].astype(F32)
    newd_ref[...] = (own_rows - scale * grad[...]) * inverse
    for c in started:
        if id(c) not in emptied:
            c.wait_send()
    for h in range(PARTS):
        for r in range(1, chips):
            over(h, r).wait_send()

        @pl.when(jnp.logical_not(home))
        def _():
            over(h, 0).wait_send()


def finish(codes_ref, newd_ref, codes_out, newd_out, sem):
    copies = [
        pltpu.make_async_copy(codes_ref, codes_out, sem.at[0]),
        pltpu.make_async_copy(newd_ref, newd_out, sem.at[1]),
    ]
    for c in copies:
        c.start()
    for c in copies:
        c.wait()


def local(groups, chips, patch_slots, slot_counts, dictionary):
    atoms_dev = chips * CORES
    slots = patch_slots[0]
    capacity, features = slots.shape
    share = features // chips
    atom_local = dictionary.shape[1]
    blocks = dictionary.reshape(chips, share, atom_local)
    span = B // CORES // PARTS
    if groups == 4:
        oth_gath = (ITERS, PARTS, groups - 1, chips, span, share)
        oth_codes = (PARTS, CORES, (groups - 1) * span, atom_local)
        oth_half = (PARTS, groups - 1, span, atom_local)
    else:
        oth_gath = oth_codes = oth_half = (8, 128)
    copies = (
        2 + 2 * ITERS * PARTS * (chips - 1) + PARTS * (3 * groups + 4 * ITERS + 4)
        + (chips - 1) * PARTS + (groups - 1) + (groups * atoms_dev - 1)
    )
    codes, newd = pl.pallas_call(
        functools.partial(kernel, groups, chips),
        out_shape=(
            pltpu.VMEM((B, atom_local), F32),
            pltpu.VMEM((share, atom_local), F32),
        ),
        in_specs=[
            pl.BlockSpec(memory_space=pltpu.SMEM),
            pl.BlockSpec(memory_space=pl.ANY),
            pl.BlockSpec(memory_space=pl.ANY),
        ],
        out_specs=(pl.BlockSpec(memory_space=pltpu.VMEM), pl.BlockSpec(memory_space=pltpu.VMEM)),
        scratch_shapes=[
            pltpu.VMEM((CORES, capacity, features), BF16),
            pltpu.VMEM((CORES, chips, share, atom_local), BF16),
            pltpu.VMEM((chips, CORES * atom_local, share), BF16),
            pltpu.VMEM((PARTS, chips, span, share), BF16),
            pltpu.VMEM((PARTS, chips - 1, span, share), BF16),
            pltpu.VMEM((ITERS, PARTS, chips, span, share), BF16),
            pltpu.VMEM((CORES, PARTS * span, atom_local), F32),
            pltpu.VMEM((PARTS, span, CORES * atom_local), BF16),
            pltpu.VMEM((PARTS, span, share), F32),
            pltpu.VMEM((ITERS, PARTS, chips - 1, span + 16, share), LINK),
            pltpu.VMEM((ITERS, PARTS, chips - 1, span + 16, share), LINK),
            pltpu.VMEM((ITERS - 1, PARTS, chips - 1, span, share), F32),
            pltpu.VMEM((ITERS - 1, PARTS, chips - 1, span, share), F32),
            pltpu.VMEM((PARTS, span, share), BF16),
            pltpu.VMEM((PARTS, groups, CORES, span, atom_local), BF16),
            pltpu.VMEM(oth_gath, BF16),
            pltpu.VMEM(oth_codes, F32),
            pltpu.VMEM(oth_half, BF16),
            pltpu.VMEM((PARTS, groups, CORES, span, share), BF16),
            pltpu.VMEM((share, atom_local), F32),
            pltpu.VMEM((2, atom_local), F32),
            pltpu.VMEM((groups - 1, 2, atom_local), F32),
            pltpu.VMEM((1, 128), F32),
            pltpu.VMEM((groups * atoms_dev - 1, 1, 128), F32),
            pltpu.SemaphoreType.DMA((copies,)),
            pltpu.SemaphoreType.DMA((copies,)),
            pltpu.SemaphoreType.DMA((PARTS, chips)),
            pltpu.SemaphoreType.DMA((PARTS, groups)),
            pltpu.SemaphoreType.DMA((2 + 2 * PARTS,)),
        ],
        compiler_params=pltpu.CompilerParams(
            collective_id=0, has_side_effects=True, vmem_limit_bytes=61 * 1024 * 1024 + 786432
        ),
    )(slot_counts[0], slots, blocks)
    codes, newd = pl.pallas_call(
        finish,
        out_shape=(
            jax.ShapeDtypeStruct((B, atom_local), F32),
            jax.ShapeDtypeStruct((share, atom_local), F32),
        ),
        in_specs=[pl.BlockSpec(memory_space=pl.ANY)] * 2,
        out_specs=(pl.BlockSpec(memory_space=pl.ANY),) * 2,
        scratch_shapes=[pltpu.SemaphoreType.DMA((2,))],
        compiler_params=pltpu.CompilerParams(vmem_limit_bytes=8 * 1024 * 1024),
    )(codes, newd)
    return (codes[None], newd)


def solution(mesh):
    groups = mesh.shape["dp"]
    chips = mesh.shape["atom"] // CORES
    assert chips == groups and chips & (chips - 1) == 0
    placed = (P("dp", "atom", None), P("dp", None), P(None, "atom"))
    return jax.shard_map(
        functools.partial(local, groups, chips),
        mesh=mesh,
        in_specs=placed,
        out_specs=(P("dp", None, "atom"), P("dp", "atom")),
        check_vma=False,
    )
```

```python
import functools
import math

import jax
import jax.numpy as jnp
from jax import lax
from jax.experimental import pallas as pl
from jax.experimental.pallas import tpu as pltpu
from jax.sharding import PartitionSpec as P

B = 256
ITERS = 3
CORES = 2
PARTS = 2
LINK = jnp.bfloat16
MESH = pl.DeviceIdType.MESH
F32 = jnp.float32
BF16 = jnp.bfloat16


def shrink(values):
    return values - jnp.clip(values, -1.0, 1.0)


def flip(index, mask, size):
    bit = 1
    while bit < size:
        if mask & bit:
            index = index + bit * (1 - 2 * ((index // bit) % 2))
        bit *= 2
    return index


def kernel(
    groups, chips, counts_ref, slots_hbm, dict_hbm, codes_out, newd_ref,
    slots, dic, dic_t, con_send, con_recv, gath, codes, half, own_part, z_send, z_recv, sent_sum, recv_sum,
    resid, half_all, oth_gath, oth_codes, oth_half, res_all, grad, col_send, col_recv, tot_send, tot_recv,
    send_sem, recv_sem, over_send, over_recv, load_sem,
):
    atoms_dev = chips * CORES
    capacity, features = slots.shape[1], slots.shape[2]
    share = features // chips
    atom_local = codes.shape[2]
    atoms_total = atom_local * atoms_dev
    span = half.shape[1]
    rows_core = PARTS * span
    lipschitz = 4.0 * (1.0 + math.sqrt(atoms_total / features)) ** 2
    g = lax.axis_index("dp")
    a = lax.axis_index("atom")
    z, k = a // CORES, a % CORES
    other = 1 - k
    sib = a + 1 - 2 * k
    mine_lanes = pl.ds(pl.multiple_of(k * atom_local, atom_local), atom_local)
    other_lanes = pl.ds(pl.multiple_of(other * atom_local, atom_local), atom_local)
    home = z == g
    near_x, near_y = g // 2 * 2 + 1 - g % 2, (g + 2) % 4
    started = []
    emptied = []

    def send(src, dst, device):
        i = len(started)
        copy = pltpu.make_async_remote_copy(
            src_ref=src, dst_ref=dst, send_sem=send_sem.at[i], recv_sem=recv_sem.at[i],
            device_id=device, device_id_type=MESH,
        )
        copy.start()
        started.append(copy)
        return copy

    def chip_of(mask):
        return flip(z, mask, chips)

    masks = list(range(chips - 1, 0, -1))

    load_slots = pltpu.make_async_copy(slots_hbm, slots.at[k], load_sem.at[0])
    load_slots.start()
    load_dict = pltpu.make_async_copy(dict_hbm, dic.at[k], load_sem.at[1])
    load_dict.start()

    barrier = pltpu.get_barrier_semaphore()
    for r in range(1, atoms_dev):
        pl.semaphore_signal(barrier, inc=1, device_id=(g, (a + r) % atoms_dev), device_id_type=MESH)
    for q in range(1, groups):
        pl.semaphore_signal(barrier, inc=1, device_id=((g + q) % groups, a), device_id_type=MESH)
        pl.semaphore_signal(
            barrier, inc=1, device_id=((g + q) % groups, g * CORES + k), device_id_type=MESH
        )

    @pl.when(jnp.logical_not(home))
    def _():
        pl.semaphore_signal(barrier, inc=1, device_id=(g, g * CORES + k), device_id_type=MESH)

    load_slots.wait()
    pl.semaphore_wait(barrier, atoms_dev - 1 + groups - 1 + chips - jnp.where(home, 1, 0))

    swap = send(slots.at[k], slots.at[k], (g, sib))
    picks = []
    slot = lax.broadcasted_iota(jnp.int32, (span, capacity), 1)
    row = lax.broadcasted_iota(jnp.int32, (span, capacity), 0) + k * rows_core
    for j in range(CORES):
        source = z * CORES + j
        start = jnp.int32(0)
        for i in range(atoms_dev):
            start = start + jnp.where(i < source, counts_ref[i], 0)
        count = counts_ref[source]
        for h in range(PARTS):
            hit = jnp.logical_and(row + h * span - start == slot, slot < count)
            picks.append(jnp.where(hit, -1.0, 0.0).astype(BF16))
    swap.wait_recv()
    load_dict.wait()
    share_dict = send(dic.at[k], dic.at[k], (g, sib))

    contributed = []
    for h in range(PARTS):
        part = jnp.dot(picks[h], slots[0], preferred_element_type=F32)
        part = part + jnp.dot(picks[PARTS + h], slots[1], preferred_element_type=F32)
        for c in range(chips):
            con_send[h, c] = part[:, c * share:(c + 1) * share].astype(BF16)
        if h:
            for c in contributed[h - 1]:
                c.wait_send()
                emptied.append(id(c))
        contributed.append([
            send(con_send.at[h, chip_of(x)], con_recv.at[h, x - 1], (g, chip_of(x) * CORES + k))
            for x in masks
        ])

    block = min(256, atom_local)
    unit = jnp.where(
        lax.broadcasted_iota(jnp.int32, (block, block), 0) == lax.broadcasted_iota(jnp.int32, (block, block), 1),
        1.0, 0.0,
    ).astype(BF16)

    def turn(j):
        for c in range(chips):
            for i in range(atom_local // block):
                rows = pl.ds(pl.multiple_of(j * atom_local + i * block, block), block)
                part = lax.dot_general(
                    unit, dic[j, c, :, i * block:(i + 1) * block], (((1,), (1,)), ((), ())),
                    preferred_element_type=F32,
                )
                dic_t[c, rows, :] = part.astype(BF16)

    def gather(t, h):
        return [
            send(gath.at[t, h, z], gath.at[t, h, z], (g, chip_of(x) * CORES + k)) for x in masks
        ]

    turn(k)
    gathers = []
    for h in range(PARTS):
        total = con_send[h, z].astype(F32)
        for c in contributed[h]:
            c.wait_recv()
        for x in masks:
            total = total + con_recv[h, x - 1].astype(F32)
        gath[0, h, z] = total.astype(BF16)
        gathers.append(gather(0, h))
    square_d = jnp.zeros((1, atom_local), F32)
    for c in range(chips):
        wide = dic[k, c].astype(F32)
        square_d = square_d + jnp.sum(wide * wide, axis=0, keepdims=True)
    share_dict.wait_recv()
    turn(other)

    tile = min(512, atom_local)

    def code(t, h, waits):
        rows = slice(h * span, (h + 1) * span)
        pairs = chips // 2

        def pair_of(i):
            return (z // 2 + i) % pairs

        def patches_of(i):
            block = gath[t, h, pl.ds(2 * pair_of(i), 2)]
            return jnp.concatenate([block[0], block[1]], axis=1)

        def product(i, x, j, cols):
            d = dic[j, pl.ds(2 * pair_of(i), 2), :, cols].reshape(2 * share, tile)
            return jnp.dot(x, d, preferred_element_type=F32)

        spots = [(j, i) for j in range(CORES) for i in range(atom_local // tile)]
        waits[-1].wait_recv()
        x = patches_of(0)
        for j, i in spots:
            cols = slice(i * tile, (i + 1) * tile)
            prod = product(0, x, j, cols)
            codes[j, rows, cols] = -prod if t == 0 else codes[j, rows, cols] - prod
        for c in waits[:-1]:
            c.wait_recv()
        if square:
            spread(t, h)
        xs = [patches_of(p) for p in range(1, pairs)]
        for j, i in spots:
            cols = slice(i * tile, (i + 1) * tile)
            new = codes[j, rows, cols]
            for p in range(1, pairs):
                new = new - product(p, xs[p - 1], j, cols)
            new = shrink(new)
            codes[j, rows, cols] = new
            half[h, :, j * atom_local + i * tile:j * atom_local + (i + 1) * tile] = new.astype(BF16)

    def known(history, t, h, slot):
        if t == 1:
            return 2.0 * history[0, h, slot]
        return 2.0 * history[t - 1, h, slot] - history[t - 2, h, slot]

    def recon_start(t, h):
        arrivals = []
        for x in masks:
            zz = chip_of(x)
            s = x - 1
            both = jnp.dot(half[h], dic_t[zz], preferred_element_type=F32)
            rows = span
            if t == 0:
                base = gath[0, h, zz].astype(F32)
                fit = jnp.sum(jnp.sum(both * base, axis=0, keepdims=True), axis=1, keepdims=True)
                norm = jnp.sum(jnp.sum(base * base, axis=0, keepdims=True), axis=1, keepdims=True)
                fit = (fit / (norm + 1e-30)).astype(LINK)
                z_send[t, h, s, span:] = jnp.broadcast_to(fit, (16, share))
                guess = fit.astype(F32) * base
                rows = span + 16
            else:
                guess = known(sent_sum, t, h, s)
            step = (both - guess).astype(LINK)
            z_send[t, h, s, :span] = step
            arrivals.append(
                (s, send(z_send.at[t, h, s, pl.ds(0, rows)], z_recv.at[t, h, s, pl.ds(0, rows)], (g, zz * CORES + k)))
            )
            if t < ITERS - 1:
                sent_sum[t, h, s] = guess + step.astype(F32)
        own_part[h] = jnp.dot(half[h], dic_t[z], preferred_element_type=F32)
        return arrivals

    def recon_end(t, h, arrivals):
        mine = own_part[h]
        negative = gath[0, h, z].astype(F32)
        for s, c in reversed(arrivals):
            c.wait_recv()
            if t == 0:
                guess = z_recv[t, h, s, span:span + 1].astype(F32) * negative
            else:
                guess = known(recv_sum, t, h, s)
            value = guess + z_recv[t, h, s, :span].astype(F32)
            if t < ITERS - 1:
                recv_sum[t, h, s] = value
            mine = mine + value
        return (mine / lipschitz + negative).astype(BF16)

    square = groups == 4
    slots_of = [near_x, near_y, groups - 1 - g] if square else []
    near = [near_x, near_y]
    half_moves, relayed, to_sib, locals_ = {}, {}, [], []

    def half_start(h):
        keep = pltpu.make_async_copy(half.at[h, :, mine_lanes], half_all.at[h, g, k], load_sem.at[2 + h])
        keep.start()
        locals_.append(keep)
        rows = pl.ds(pl.multiple_of(k * rows_core + h * span, span), span)
        keep = pltpu.make_async_copy(
            codes.at[k, pl.ds(h * span, span)], codes_out.at[rows], load_sem.at[2 + PARTS + h]
        )
        keep.start()
        locals_.append(keep)
        for q in ([] if square else range(1, groups)):
            peer = (g + q) % groups
            half_moves[h, q] = (
                send(half.at[h, :, mine_lanes], half_all.at[h, g, k], (peer, a)),
                send(half.at[h, :, other_lanes], half_all.at[h, g, k], (peer, sib)),
            )
        to_sib.append(send(half.at[h, :, other_lanes], half_all.at[h, g, k], (g, sib)))

    def codes_start(h):
        rows = pl.ds(pl.multiple_of(k * rows_core + h * span, span), span)
        to_sib.append(send(codes.at[other, pl.ds(h * span, span)], codes_out.at[rows], (g, sib)))

    def spread(t, h):
        half_moves[t, h] = [send(gath.at[t, h], oth_gath.at[t, h, i], (near[i], a)) for i in range(2)]

    def relay(t, h):
        relayed[t, h] = []
        for p in range(2):
            half_moves[t, h][1 - p].wait_recv()
            blocks = pl.ds(p * (chips // 2), chips // 2)
            relayed[t, h].append(
                send(oth_gath.at[t, h, 1 - p, blocks], oth_gath.at[t, h, 2, blocks], (near[p], a))
            )

    def others(t, h):
        last = t == ITERS - 1
        for c in relayed[t, h]:
            c.wait_recv()
        x = jnp.concatenate(
            [
                jnp.concatenate([oth_gath[t, h, i, c] for c in range(chips)], axis=1)
                for i in range(groups - 1)
            ],
            axis=0,
        )
        for j in (other, k):
            for i in range(atom_local // 256):
                cols = slice(i * 256, (i + 1) * 256)
                d = dic[j, :, :, cols].reshape(features, 256)
                prod = jnp.dot(x, d, preferred_element_type=F32)
                new = shrink(-prod if t == 0 else oth_codes[h, j, :, cols] - prod)
                if not last:
                    oth_codes[h, j, :, cols] = new
                    continue
                new = new.astype(BF16)
                for q in range(groups - 1):
                    rows = new[q * span:(q + 1) * span]
                    if j is k:
                        half_all[h, slots_of[q], k, :, cols] = rows
                    else:
                        oth_half[h, q, :, cols] = rows
            if last and j is not k:
                for q in range(groups - 1):
                    to_sib.append(send(oth_half.at[h, q], half_all.at[h, slots_of[q], k], (g, sib)))

    def half_end(h):
        if square:
            others(ITERS - 1, h)
        else:
            for q in range(1, groups):
                for c in half_moves[h, q]:
                    c.wait_recv()

    def over(h, r):
        zz = (z + r) % chips
        return pltpu.make_async_remote_copy(
            src_ref=resid.at[h], dst_ref=res_all.at[h, g, k], send_sem=over_send.at[h, r],
            recv_sem=over_recv.at[h, g], device_id=(z, zz * CORES + k), device_id_type=MESH,
        )

    def over_arrival(h, q):
        return pltpu.make_async_remote_copy(
            src_ref=resid.at[h], dst_ref=res_all.at[h, q, k], send_sem=over_send.at[h, 0],
            recv_sem=over_recv.at[h, q], device_id=(g, sib), device_id_type=MESH,
        )

    def over_start(h, value):
        resid[h] = value
        for r in range(1, chips):
            over(h, r).start()

        @pl.when(jnp.logical_not(home))
        def _():
            over(h, 0).start()

        @pl.when(home)
        def _():
            res_all[h, g, k] = value

    def over_end(h):
        for p in range(groups):
            q = (g + p) % groups
            if p:
                over_arrival(h, q).wait_recv()
            else:
                @pl.when(jnp.logical_not(home))
                def _():
                    over_arrival(h, q).wait_recv()
            to_sib.append(send(res_all.at[h, q, k], res_all.at[h, q, k], (g, sib)))

    for t in range(ITERS):
        last = t == ITERS - 1
        arrivals = []
        for h in range(PARTS):
            code(t, h, gathers[h])
            if last:
                half_start(h)
            arrivals.append(recon_start(t, h))
        gathers = []
        for h in range(PARTS):
            value = recon_end(t, h, arrivals[h])
            if last:
                over_start(h, value)
                codes_start(h)
                if square and h < PARTS - 1:
                    relay(t, h)
            else:
                gath[t + 1, h, z] = value
                gathers.append(gather(t + 1, h))
                if square and t == 0 and h == 0:
                    relay(t, 0)
        if square:
            for h in range(PARTS):
                if t == 1 and h == 0:
                    relay(t, 0)
                if t:
                    others(t - 1, h)
                if last and h == 0:
                    relay(t, PARTS - 1)
            for h in range(PARTS):
                if not last and h:
                    relay(t, h)

    done = 0
    cols_tile = min(256, atom_local)
    depth = groups * CORES * span
    for h in range(PARTS):
        half_end(h)
        over_end(h)
        for c in to_sib[done:]:
            c.wait_recv()
        done = len(to_sib)
        if h == 0:
            for c in locals_:
                c.wait()
        left = res_all[h].reshape(depth, share)
        for i in range(atom_local // cols_tile):
            cols = slice(i * cols_tile, (i + 1) * cols_tile)
            right = half_all[h, :, :, :, cols].reshape(depth, cols_tile)
            prod = lax.dot_general(left, right, (((0,), (0,)), ((), ())), preferred_element_type=F32)
            if h > 0:
                prod = grad[:, cols] + prod
            grad[:, cols] = prod
            if h == PARTS - 1:
                d = dic[k, g, :, cols].astype(F32)
                col_send[0:1, cols] = jnp.sum(d * prod, axis=0, keepdims=True)
                col_send[1:2, cols] = jnp.sum(prod * prod, axis=0, keepdims=True)

    total = jnp.sum(col_send[1:2], axis=1, keepdims=True)
    tot_send[...] = jnp.broadcast_to(total, tot_send.shape)
    moves = [send(col_send, col_recv.at[q - 1], ((g + q) % groups, a)) for q in range(1, groups)]
    everyone = [(q, r) for q in range(groups) for r in range(atoms_dev) if q or r]
    everyone.sort(key=lambda p: abs(p[1] - atoms_dev // 2))
    totals = [
        send(tot_send, tot_recv.at[i], ((g + q) % groups, (a + r) % atoms_dev))
        for i, (q, r) in enumerate(everyone)
    ]
    column = col_send[...]
    for q in range(1, groups):
        moves[q - 1].wait_recv()
        column = column + col_recv[q - 1]
    cross, square_g = column[0:1], column[1:2]
    for c in totals:
        c.wait_recv()
    line = tot_send[...] + jnp.sum(tot_recv[...], axis=0)
    scale = (0.5 * math.sqrt(atoms_total)) / jnp.sqrt(line[0:1, 0:1])
    norm = square_d + scale * (scale * square_g - 2.0 * cross)
    norm = jnp.where(scale == 0.0, square_d, jnp.maximum(norm, 0.0))
    inverse = 1.0 / jnp.sqrt(norm + 1e-06)
    own_rows = dic[k, g].astype(F32)
    newd_ref[...] = (own_rows - scale * grad[...]) * inverse
    for c in started:
        if id(c) not in emptied:
            c.wait_send()
    for h in range(PARTS):
        for r in range(1, chips):
            over(h, r).wait_send()

        @pl.when(jnp.logical_not(home))
        def _():
            over(h, 0).wait_send()


def finish(codes_ref, newd_ref, codes_out, newd_out, sem):
    copies = [
        pltpu.make_async_copy(codes_ref, codes_out, sem.at[0]),
        pltpu.make_async_copy(newd_ref, newd_out, sem.at[1]),
    ]
    for c in copies:
        c.start()
    for c in copies:
        c.wait()


def local(groups, chips, patch_slots, slot_counts, dictionary):
    atoms_dev = chips * CORES
    slots = patch_slots[0]
    capacity, features = slots.shape
    share = features // chips
    atom_local = dictionary.shape[1]
    blocks = dictionary.reshape(chips, share, atom_local)
    span = B // CORES // PARTS
    if groups == 4:
        oth_gath = (ITERS, PARTS, groups - 1, chips, span, share)
        oth_codes = (PARTS, CORES, (groups - 1) * span, atom_local)
        oth_half = (PARTS, groups - 1, span, atom_local)
    else:
        oth_gath = oth_codes = oth_half = (8, 128)
    copies = (
        2 + 2 * ITERS * PARTS * (chips - 1) + PARTS * (3 * groups + 4 * ITERS + 4)
        + (chips - 1) * PARTS + (groups - 1) + (groups * atoms_dev - 1)
    )
    codes, newd = pl.pallas_call(
        functools.partial(kernel, groups, chips),
        out_shape=(
            pltpu.VMEM((B, atom_local), F32),
            pltpu.VMEM((share, atom_local), F32),
        ),
        in_specs=[
            pl.BlockSpec(memory_space=pltpu.SMEM),
            pl.BlockSpec(memory_space=pl.ANY),
            pl.BlockSpec(memory_space=pl.ANY),
        ],
        out_specs=(pl.BlockSpec(memory_space=pltpu.VMEM), pl.BlockSpec(memory_space=pltpu.VMEM)),
        scratch_shapes=[
            pltpu.VMEM((CORES, capacity, features), BF16),
            pltpu.VMEM((CORES, chips, share, atom_local), BF16),
            pltpu.VMEM((chips, CORES * atom_local, share), BF16),
            pltpu.VMEM((PARTS, chips, span, share), BF16),
            pltpu.VMEM((PARTS, chips - 1, span, share), BF16),
            pltpu.VMEM((ITERS, PARTS, chips, span, share), BF16),
            pltpu.VMEM((CORES, PARTS * span, atom_local), F32),
            pltpu.VMEM((PARTS, span, CORES * atom_local), BF16),
            pltpu.VMEM((PARTS, span, share), F32),
            pltpu.VMEM((ITERS, PARTS, chips - 1, span + 16, share), LINK),
            pltpu.VMEM((ITERS, PARTS, chips - 1, span + 16, share), LINK),
            pltpu.VMEM((ITERS - 1, PARTS, chips - 1, span, share), F32),
            pltpu.VMEM((ITERS - 1, PARTS, chips - 1, span, share), F32),
            pltpu.VMEM((PARTS, span, share), BF16),
            pltpu.VMEM((PARTS, groups, CORES, span, atom_local), BF16),
            pltpu.VMEM(oth_gath, BF16),
            pltpu.VMEM(oth_codes, F32),
            pltpu.VMEM(oth_half, BF16),
            pltpu.VMEM((PARTS, groups, CORES, span, share), BF16),
            pltpu.VMEM((share, atom_local), F32),
            pltpu.VMEM((2, atom_local), F32),
            pltpu.VMEM((groups - 1, 2, atom_local), F32),
            pltpu.VMEM((1, 128), F32),
            pltpu.VMEM((groups * atoms_dev - 1, 1, 128), F32),
            pltpu.SemaphoreType.DMA((copies,)),
            pltpu.SemaphoreType.DMA((copies,)),
            pltpu.SemaphoreType.DMA((PARTS, chips)),
            pltpu.SemaphoreType.DMA((PARTS, groups)),
            pltpu.SemaphoreType.DMA((2 + 2 * PARTS,)),
        ],
        compiler_params=pltpu.CompilerParams(
            collective_id=0, has_side_effects=True, vmem_limit_bytes=61 * 1024 * 1024 + 786432
        ),
    )(slot_counts[0], slots, blocks)
    codes, newd = pl.pallas_call(
        finish,
        out_shape=(
            jax.ShapeDtypeStruct((B, atom_local), F32),
            jax.ShapeDtypeStruct((share, atom_local), F32),
        ),
        in_specs=[pl.BlockSpec(memory_space=pl.ANY)] * 2,
        out_specs=(pl.BlockSpec(memory_space=pl.ANY),) * 2,
        scratch_shapes=[pltpu.SemaphoreType.DMA((2,))],
        compiler_params=pltpu.CompilerParams(vmem_limit_bytes=8 * 1024 * 1024),
    )(codes, newd)
    return (codes[None], newd)


def solution(mesh):
    groups = mesh.shape["dp"]
    chips = mesh.shape["atom"] // CORES
    assert chips == groups and chips & (chips - 1) == 0
    placed = (P("dp", "atom", None), P("dp", None), P(None, "atom"))
    return jax.shard_map(
        functools.partial(local, groups, chips),
        mesh=mesh,
        in_specs=placed,
        out_specs=(P("dp", None, "atom"), P("dp", "atom")),
        check_vma=False,
    )
```
